256 devices in a mesh: dp: 2 (over y_lo), seq: 128 (over x, y_hi, z, core).
Axes of the slice: x: 4, y: 4 (y_hi: 2, y_lo: 2; y = y_hi * 2 + y_lo), z: 8, core: 2. Of those that a mesh axis runs over, the one named last changes fastest.
Arguments:
- tokens: bfloat16 [2, 128, 512, 384], P('dp', 'seq'), may hold values from -6 to 6
- cotangent: bfloat16 [2, 128, 512, 384], P('dp', 'seq'), may hold values from -6 to 6
- wqkv_spatial: bfloat16 [384, 1152], replicated, may hold values from -12.5 to 12.5
- wo_spatial: bfloat16 [384, 384], replicated, may hold values from -0.3125 to 0.3125
- wqkv_temporal: bfloat16 [384, 1152], replicated, may hold values from -12.5 to 12.5
- wo_temporal: bfloat16 [384, 384], replicated, may hold values from -0.3125 to 0.3125
Outputs:
- token_grad: bfloat16 [2, 128, 512, 384], P('dp', 'seq')
- grad_wqkv_spatial: float32 [384, 1152], P(None, 'seq')
- grad_wo_spatial: float32 [384, 384], P(None, 'seq')
- grad_wqkv_temporal: float32 [384, 1152], P(None, 'seq')
- grad_wo_temporal: float32 [384, 384], P(None, 'seq')
The draws below stay inside these ranges and needn't reach their ends.
All inputs are finite; a program needn't handle non-finite values.
Results may differ from the reference program's by a relative error of at most 0.015.
Values may be sent and summed in bfloat16 or wider, within the bound.
No kernel may reach another device: no remote copies, remote signals or barrier semaphores. Data moves between devices by JAX's collectives and lax.ppermute only.
A program may use at most 64 MiB of HBM per device.

```python
import jax
import jax.numpy as jnp
from jax import lax

D = 384
HEADS = 6
FRAMES = 128
PATCHES = 512
CLIPS = 2


def projection(key):
    matrix = jnp.clip(jax.random.normal(key, (D, 3 * D), jnp.float32), -4.0, 4.0) * D ** (-0.5)
    return matrix.astype(jnp.bfloat16)


def draw_wqkv_spatial(key, part):
    return projection(jax.random.fold_in(key, 11))


def draw_wqkv_temporal(key, part):
    return projection(jax.random.fold_in(key, 23))


def block_levels(key, extent, cuts, low, largest):
    loudness, own = 1.0, jax.random.fold_in(key, 6)
    for dim, shards_of in cuts:
        draws = jnp.exp(jax.random.uniform(jax.random.fold_in(own, dim), (shards_of,), jnp.float32, low / len(cuts), largest / len(cuts)))
        loudness = loudness * jnp.repeat(draws, extent[dim] // shards_of).reshape([-1 if axis == dim else 1 for axis in range(len(extent))])
    return loudness


def noise(key, extent, scale, limit, shards=(), kind=jnp.bfloat16):
    array = scale * jax.random.normal(key, extent, jnp.float32)
    if shards:
        array = array * block_levels(key, extent, shards, -0.22, 0.18)
    return jnp.clip(array, -limit, limit).astype(kind)


def setup_inputs(seed: int = 0) -> dict:
    arg_keys = jax.random.split(jax.random.key(seed), 7)
    tokens = noise(arg_keys[0], (CLIPS, FRAMES, PATCHES, D), 1.0, 6.0, ((0, 2), (1, 128)))
    cotangent = noise(arg_keys[1], (CLIPS, FRAMES, PATCHES, D), 1.0, 6.0, ((0, 2), (1, 128)))
    wqkv_spatial = draw_wqkv_spatial(jax.random.fold_in(arg_keys[6], 71), 0)
    wo_spatial = noise(arg_keys[3], (D, D), D ** -0.5, 0.3125)
    wqkv_temporal = draw_wqkv_temporal(jax.random.fold_in(arg_keys[6], 71), 0)
    wo_temporal = noise(arg_keys[5], (D, D), D ** -0.5, 0.3125)
    return {"tokens": tokens, "cotangent": cotangent, "wqkv_spatial": wqkv_spatial, "wo_spatial": wo_spatial, "wqkv_temporal": wqkv_temporal, "wo_temporal": wo_temporal}


def product(pattern, left, right):
    return jnp.einsum(pattern, left.astype(jnp.float32), right.astype(jnp.float32))

def normalize(values):
    average = lax.optimization_barrier(jnp.mean(values, -1, keepdims=True))
    centered = values - average
    spread = lax.optimization_barrier(jnp.mean(centered * centered, -1, keepdims=True))
    inverse = lax.rsqrt(spread + 1e-06)
    return (centered * inverse, inverse)

def normalize_back(scaled, inverse, upstream):
    return inverse * (upstream - lax.optimization_barrier(jnp.mean(upstream, -1, keepdims=True)) - scaled * lax.optimization_barrier(jnp.mean(upstream * scaled, -1, keepdims=True)))

def softmax_rounded(queries, key_rows):
    factor = queries.shape[-1] ** (-0.5)
    scores = product('bshe,bthe->bhst', queries, key_rows) * factor
    return jax.nn.softmax(scores, axis=-1).astype(jnp.bfloat16)

def attend(queries, key_rows, values):
    probs = softmax_rounded(queries, key_rows)
    return product('bhst,bthe->bshe', probs, values).astype(jnp.bfloat16)

def attend_back(queries, key_rows, values, upstream):
    factor = queries.shape[-1] ** (-0.5)
    probs = softmax_rounded(queries, key_rows)
    weights = probs.astype(jnp.float32)
    prob_grad = product('bshe,bthe->bhst', upstream, values)
    score_grad = (weights * (prob_grad - lax.optimization_barrier(jnp.sum(weights * prob_grad, -1, keepdims=True))) * factor).astype(jnp.bfloat16)
    query_grad = product('bhst,bthe->bshe', score_grad, key_rows)
    key_grad = product('bhst,bshe->bthe', score_grad, queries)
    value_grad = product('bhst,bshe->bthe', probs, upstream)
    return jnp.concatenate([query_grad, key_grad, value_grad], axis=2)

def grouped(function, arrays, group):
    total_rows = arrays[0].shape[0]
    shaped = tuple((member.reshape((total_rows // group, group) + member.shape[1:]) for member in arrays))
    result = lax.map(lambda bundle: function(*bundle), shaped)
    return result.reshape((total_rows,) + result.shape[2:])

def split_heads(combined):
    shape = combined.shape
    parted = combined.reshape(shape[:-1] + (3, HEADS, shape[-1] // (3 * HEADS)))
    return (parted[..., 0, :, :], parted[..., 1, :, :], parted[..., 2, :, :])

def to_frames(tensor):
    return tensor.reshape((-1,) + tensor.shape[2:])

def to_patches(tensor):
    shape = tensor.shape
    moved = jnp.transpose(tensor, (0, 2, 1, 3, 4))
    return moved.reshape((shape[0] * shape[2], shape[1]) + shape[3:])

def from_patches(tensor, clip_count, patch_count):
    shape = tensor.shape
    joined = tensor.reshape((clip_count, patch_count, shape[1], shape[2] * shape[3]))
    return jnp.transpose(joined, (0, 2, 1, 3))

def reference(tokens, cotangent, wqkv_spatial, wo_spatial, wqkv_temporal, wo_temporal):
    clip_count, frame_count, patch_count, model_width = tokens.shape
    inputs = tokens.astype(jnp.float32)
    scaled_s, inverse_s = normalize(inputs)
    normed_s = scaled_s.astype(jnp.bfloat16)
    combined_s = jnp.dot(normed_s, wqkv_spatial, preferred_element_type=jnp.float32).astype(jnp.bfloat16)
    queries_s, keys_s, values_s = [to_frames(member) for member in split_heads(combined_s)]
    attended_s = grouped(attend, (queries_s, keys_s, values_s), 1).reshape(tokens.shape)
    stream = (inputs + jnp.dot(attended_s, wo_spatial, preferred_element_type=jnp.float32)).astype(jnp.bfloat16)
    scaled_t, inverse_t = normalize(stream.astype(jnp.float32))
    normed_t = scaled_t.astype(jnp.bfloat16)
    combined_t = jnp.dot(normed_t, wqkv_temporal, preferred_element_type=jnp.float32).astype(jnp.bfloat16)
    queries_t, keys_t, values_t = [to_patches(member) for member in split_heads(combined_t)]
    attended_t = from_patches(grouped(attend, (queries_t, keys_t, values_t), 8), clip_count, patch_count)
    grad_wo_t = product('cfpd,cfpe->de', attended_t, cotangent)
    upstream_t = jnp.dot(cotangent, wo_temporal.T, preferred_element_type=jnp.float32).astype(jnp.bfloat16)
    upstream_t = to_patches(upstream_t.reshape(queries_s.shape[:0] + (clip_count, frame_count, patch_count, HEADS, model_width // HEADS)))
    combined_grad_t = from_patches(grouped(attend_back, (queries_t, keys_t, values_t, upstream_t), 8), clip_count, patch_count).astype(jnp.bfloat16)
    grad_wqkv_t = product('cfpd,cfpe->de', normed_t, combined_grad_t)
    input_grad_t = jnp.dot(combined_grad_t, wqkv_temporal.T, preferred_element_type=jnp.float32)
    branch_t = normalize_back(scaled_t, inverse_t, input_grad_t).astype(jnp.bfloat16)
    stream_grad = (cotangent.astype(jnp.float32) + branch_t.astype(jnp.float32)).astype(jnp.bfloat16)
    grad_wo_s = product('cfpd,cfpe->de', attended_s, stream_grad)
    upstream_s = jnp.dot(stream_grad, wo_spatial.T, preferred_element_type=jnp.float32).astype(jnp.bfloat16)
    upstream_s = upstream_s.reshape(queries_s.shape)
    combined_grad_s = grouped(attend_back, (queries_s, keys_s, values_s, upstream_s), 1)
    combined_grad_s = combined_grad_s.reshape(combined_s.shape).astype(jnp.bfloat16)
    grad_wqkv_s = product('cfpd,cfpe->de', normed_s, combined_grad_s)
    input_grad_s = jnp.dot(combined_grad_s, wqkv_spatial.T, preferred_element_type=jnp.float32)
    token_grad = (stream_grad.astype(jnp.float32) + normalize_back(scaled_s, inverse_s, input_grad_s)).astype(jnp.bfloat16)
    factor = (clip_count * frame_count * patch_count) ** (-0.5)
    return (token_grad, grad_wqkv_s * factor, grad_wo_s * factor, grad_wqkv_t * factor, grad_wo_t * factor)
```

```python
import jax
import jax.numpy as jnp
from jax import lax
from jax.sharding import PartitionSpec as P

HEADS = 6


def product(pattern, left, right):
    return jnp.einsum(pattern, left, right, preferred_element_type=jnp.float32)


def normalize(values):
    average = jnp.mean(values, -1, keepdims=True)
    centered = values - average
    spread = jnp.mean(centered * centered, -1, keepdims=True)
    inverse = lax.rsqrt(spread + 1e-06)
    return (centered * inverse, inverse)


def normalize_back(scaled, inverse, upstream):
    return inverse * (
        upstream
        - jnp.mean(upstream, -1, keepdims=True)
        - scaled * jnp.mean(upstream * scaled, -1, keepdims=True)
    )


def patterns(layout):
    key_layout = layout.replace("s", "t")
    batch_letters = "".join((letter for letter in layout if letter not in "she"))
    return (key_layout, batch_letters + "hst")


def attend_block(queries, key_rows, values, layout):
    key_layout, score_layout = patterns(layout)
    factor = queries.shape[-1] ** (-0.5)
    scores = product(layout + "," + key_layout + "->" + score_layout, queries, key_rows) * factor
    probs = jax.nn.softmax(scores, axis=-1).astype(jnp.bfloat16)
    output = product(score_layout + "," + key_layout + "->" + layout, probs, values).astype(
        jnp.bfloat16
    )
    return (output, probs)


def attend_grad(queries, key_rows, values, upstream, probs, layout):
    key_layout, score_layout = patterns(layout)
    factor = queries.shape[-1] ** (-0.5)
    prob_grad = product(layout + "," + key_layout + "->" + score_layout, upstream, values)
    weights = probs.astype(jnp.float32)
    score_grad = (
        weights * (prob_grad - jnp.sum(weights * prob_grad, -1, keepdims=True)) * factor
    ).astype(jnp.bfloat16)
    query_grad = product(score_layout + "," + key_layout + "->" + layout, score_grad, key_rows)
    key_grad = product(score_layout + "," + layout + "->" + key_layout, score_grad, queries)
    value_grad = product(score_layout + "," + layout + "->" + key_layout, probs, upstream)
    return (query_grad, key_grad, value_grad)


def split_heads(combined):
    shape = combined.shape
    parted = combined.reshape(shape[:-1] + (3, HEADS, shape[-1] // (3 * HEADS)))
    return (parted[..., 0, :, :], parted[..., 1, :, :], parted[..., 2, :, :])


def frame_rows(tensor):
    return tensor.reshape((-1,) + tensor.shape[2:])


SEQ = (("x", 4), ("yh", 2), ("z", 8), ("core", 2))


def seq_size():
    return lax.axis_size("seq")


def place(name):
    stride = 1
    for member, size in reversed(SEQ):
        if member == name:
            return stride, size
        stride *= size


def coordinate(name):
    stride, size = place(name)
    return lax.axis_index("seq") // stride % size


def shift(array, name, step):
    stride, size = place(name)
    pairs = []
    for index in range(seq_size()):
        at = index // stride % size
        pairs.append((index, index + ((at + step) % size - at) * stride))
    return lax.ppermute(array, "seq", pairs)


def stage(chunks, name):
    size = chunks.shape[0]
    here = coordinate(name)
    total = lax.dynamic_index_in_dim(chunks, here, 0, keepdims=False).astype(jnp.float32)
    for step in range(1, size):
        part = lax.dynamic_index_in_dim(chunks, (here + step) % size, 0, keepdims=False)
        total = total + shift(part, name, step).astype(jnp.float32)
    return total


def reduce_slabs(slabs):
    sizes = [size for _, size in SEQ]
    chunks = slabs.reshape(*sizes, *slabs.shape[1:])
    chunks = stage(jnp.moveaxis(chunks, 3, 0), "core").astype(jnp.bfloat16)
    chunks = stage(chunks, "x").astype(jnp.bfloat16)
    chunks = stage(jnp.moveaxis(chunks, 1, 0), "z").astype(jnp.bfloat16)
    mine = stage(chunks, "yh").astype(jnp.bfloat16)
    other = lax.ppermute(mine, "dp", [(0, 1), (1, 0)])
    return mine.astype(jnp.float32) + other.astype(jnp.float32)


def on_device(tokens, cotangent, wqkv_spatial, wo_spatial, wqkv_temporal, wo_temporal):
    clip_count, frame_local, patch_count, model_width = tokens.shape
    head_width = model_width // HEADS
    block_rows = min(512, patch_count)
    inputs = tokens.astype(jnp.float32)
    scaled_s, inverse_s = normalize(inputs)
    normed_s = scaled_s.astype(jnp.bfloat16)
    combined_s = jnp.dot(normed_s, wqkv_spatial, preferred_element_type=jnp.float32).astype(
        jnp.bfloat16
    )
    queries_s, keys_s, values_s = [frame_rows(member) for member in split_heads(combined_s)]
    output, probs = attend_block(queries_s, keys_s, values_s, "bshe")
    outputs_s = [output]
    probs_s = [probs]
    attended_s = jnp.concatenate(outputs_s, 1).reshape(tokens.shape)
    stream = (inputs + jnp.dot(attended_s, wo_spatial, preferred_element_type=jnp.float32)).astype(
        jnp.bfloat16
    )
    stream_t, upstream_out = (
        lax.all_to_all(stream, "seq", split_axis=2, concat_axis=1, tiled=True),
        lax.all_to_all(cotangent, "seq", split_axis=2, concat_axis=1, tiled=True),
    )
    scaled_t, inverse_t = normalize(stream_t.astype(jnp.float32))
    normed_t = scaled_t.astype(jnp.bfloat16)
    combined_t = jnp.dot(normed_t, wqkv_temporal, preferred_element_type=jnp.float32).astype(
        jnp.bfloat16
    )
    queries_t, keys_t, values_t = split_heads(combined_t)
    attended_t, probs_t = attend_block(queries_t, keys_t, values_t, "csphe")
    attended_t = attended_t.reshape(stream_t.shape)
    factor = (
        clip_count * frame_local * patch_count * lax.axis_size("dp") * lax.axis_size("seq")
    ) ** (-0.5)
    grad_wo_t = product("cfpd,cfpe->de", attended_t, upstream_out) * factor
    head_grad_t = (
        product("cfpe,de->cfpd", upstream_out, wo_temporal)
        .astype(jnp.bfloat16)
        .reshape(queries_t.shape)
    )
    query_grad, key_grad, value_grad = attend_grad(
        queries_t, keys_t, values_t, head_grad_t, probs_t, "csphe"
    )
    combined_grad_t = (
        jnp.concatenate([query_grad, key_grad, value_grad], 3)
        .astype(jnp.bfloat16)
        .reshape(combined_t.shape)
    )
    grad_wqkv_t = product("cfpd,cfpe->de", normed_t, combined_grad_t) * factor
    input_grad_t = product("cfpe,de->cfpd", combined_grad_t, wqkv_temporal)
    branch_t = normalize_back(scaled_t, inverse_t, input_grad_t).astype(jnp.bfloat16)
    branch_s = lax.all_to_all(branch_t, "seq", split_axis=1, concat_axis=2, tiled=True)
    stream_grad = (cotangent.astype(jnp.float32) + branch_s.astype(jnp.float32)).astype(
        jnp.bfloat16
    )
    grad_wo_s = product("cfpd,cfpe->de", attended_s, stream_grad) * factor
    head_grad_s = frame_rows(
        product("cfpe,de->cfpd", stream_grad, wo_spatial)
        .astype(jnp.bfloat16)
        .reshape(tokens.shape[:3] + (HEADS, head_width))
    )
    key_total = jnp.zeros(keys_s.shape, jnp.float32)
    value_total = jnp.zeros(values_s.shape, jnp.float32)
    query_parts = []
    for number, offset in enumerate(range(0, patch_count, block_rows)):
        query_grad, key_grad, value_grad = attend_grad(
            queries_s, keys_s, values_s, head_grad_s, probs_s[number], "bshe"
        )
        query_parts.append(query_grad)
        key_total = key_total + key_grad
        value_total = value_total + value_grad
    combined_grad_s = jnp.concatenate([jnp.concatenate(query_parts, 1), key_total, value_total], 2)
    combined_grad_s = combined_grad_s.astype(jnp.bfloat16).reshape(combined_s.shape)
    grad_wqkv_s = product("cfpd,cfpe->de", normed_s, combined_grad_s) * factor
    input_grad_s = product("cfpe,de->cfpd", combined_grad_s, wqkv_spatial)
    token_grad = (
        stream_grad.astype(jnp.float32) + normalize_back(scaled_s, inverse_s, input_grad_s)
    ).astype(jnp.bfloat16)
    gradients = (grad_wqkv_s, grad_wo_s, grad_wqkv_t, grad_wo_t)
    slabs = jnp.concatenate(
        [
            member.T.reshape(seq_size(), -1, model_width).astype(jnp.bfloat16)
            for member in gradients
        ],
        1,
    )
    own = reduce_slabs(slabs)
    shares, start = [], 0
    for member in gradients:
        count = member.shape[1] // seq_size()
        shares.append(own[start : start + count].T)
        start += count
    return (token_grad, shares[0], shares[1], shares[2], shares[3])


def solution(mesh):
    in_specs = (P("dp", "seq", None, None), P("dp", "seq", None, None), P(), P(), P(), P())
    out_specs = (
        P("dp", "seq", None, None),
        P(None, "seq"),
        P(None, "seq"),
        P(None, "seq"),
        P(None, "seq"),
    )
    return jax.shard_map(
        on_device, mesh=mesh, in_specs=in_specs, out_specs=out_specs, check_vma=False
    )
```

```python
import functools

import jax
import jax.numpy as jnp
import numpy as np
from jax import lax
from jax.experimental import pallas as pl
from jax.experimental.pallas import tpu as pltpu
from jax.sharding import PartitionSpec as P

HEADS = 6
F32 = jnp.float32
B16 = jnp.bfloat16
NN = (((1,), (0,)), ((), ()))
NT = (((1,), (1,)), ((), ()))
TN = (((0,), (0,)), ((), ()))
VM = pl.BlockSpec(memory_space=pltpu.VMEM)


def mm(left, right, dims=NN):
    return lax.dot_general(left, right, dims, preferred_element_type=F32)


def normalize(values):
    average = jnp.mean(values, -1, keepdims=True)
    centered = values - average
    spread = jnp.mean(centered * centered, -1, keepdims=True)
    inverse = lax.rsqrt(spread + 1e-06)
    return centered * inverse, inverse


def normalize_back(scaled, inverse, upstream):
    return inverse * (
        upstream
        - jnp.mean(upstream, -1, keepdims=True)
        - scaled * jnp.mean(upstream * scaled, -1, keepdims=True)
    )


def one_head(block, sub, half, rows_axis):
    at = lax.broadcasted_iota(jnp.int32, block.shape, rows_axis)
    keep = (at < half) if sub == 0 else (at >= half)
    return jnp.where(keep, block, jnp.zeros_like(block))


def spatial_forward_kernel(tok_ref, w_ref, wo_ref, out_ref, comb_ref, att_ref, probs_ref):
    width = tok_ref.shape[-1]
    hw = width // HEADS
    x = tok_ref[...].astype(F32)
    scaled, _ = normalize(x)
    comb = mm(scaled.astype(B16), w_ref[...]).astype(B16)
    comb_ref[...] = comb
    qt = (comb[:, :width] * (hw ** -0.5)).T
    vt = comb[:, 2 * width :].T
    parts = []
    for pair in range(HEADS // 2):
        at = pair * 2 * hw
        keys = comb[:, width + at : width + at + 2 * hw]
        for sub in range(2):
            head = 2 * pair + sub
            q = one_head(qt[at : at + 2 * hw], sub, hw, 0)
            s = mm(keys, q)
            e = jnp.exp(s - jnp.max(s, 0, keepdims=True))
            p = (e * (1.0 / jnp.sum(e, 0, keepdims=True))).astype(B16)
            probs_ref[head] = p
            parts.append(mm(vt[head * hw : (head + 1) * hw], p).astype(B16))
    att = jnp.concatenate(parts, 0).T
    att_ref[...] = att
    out = (x + mm(att, wo_ref[...])).astype(B16)
    out_ref[...] = out.reshape(out_ref.shape)


def spatial_forward(tokens, w, wo, out_shape):
    rows, width = tokens.shape
    return pl.pallas_call(
        spatial_forward_kernel,
        out_shape=(
            jax.ShapeDtypeStruct(out_shape, B16),
            jax.ShapeDtypeStruct((rows, 3 * width), B16),
            jax.ShapeDtypeStruct((rows, width), B16),
            jax.ShapeDtypeStruct((HEADS, rows, rows), B16),
        ),
        in_specs=[VM] * 3,
        out_specs=(VM,) * 4,
        compiler_params=pltpu.CompilerParams(vmem_limit_bytes=16 << 20),
        name="spatial_forward",
    )(tokens, w, wo)


def softmax_rows(scores):
    e = jnp.exp(scores - jnp.max(scores, 0, keepdims=True))
    return (e * (1.0 / jnp.sum(e, 0, keepdims=True))).astype(B16)


def score_back(probs, prob_grad):
    weights = probs.astype(F32)
    total = jnp.sum(weights * prob_grad, 0, keepdims=True)
    return (weights * (prob_grad - total)).astype(B16)


def both_heads(block, half, rows_axis, join_axis):
    return jnp.concatenate(
        [one_head(block, 0, half, rows_axis), one_head(block, 1, half, rows_axis)], join_axis
    )


def regroup(count, inner, outer):
    row = lax.broadcasted_iota(jnp.int32, (count, count), 0)
    column = lax.broadcasted_iota(jnp.int32, (count, count), 1)
    source = (row & (inner - 1)) * outer + lax.shift_right_logical(row, inner.bit_length() - 1)
    return (column == source).astype(F32).astype(B16)


def temporal_kernel(
    st_ref, ct_ref, w_ref, wo_ref, branch_ref, normed_ref, cot_ref, att_ref, dct_ref
):
    frames, patches, width = st_ref.shape
    rows = frames * patches
    hw = width // HEADS
    gather = regroup(rows, frames, patches)
    x = mm(gather, st_ref[...].reshape(rows, width))
    cot = mm(gather, ct_ref[...].reshape(rows, width)).astype(B16)
    cot_ref[...] = cot
    scaled, inverse = normalize(x)
    normed = scaled.astype(B16)
    normed_ref[...] = normed
    comb = mm(normed, w_ref[...]).astype(B16)
    g = mm(cot, wo_ref[...], NT).astype(B16)
    q = comb[:, :width] * (hw ** -0.5)
    k = comb[:, width : 2 * width]
    v = comb[:, 2 * width :]
    qt, kt, vt, gt = q.T, k.T, v.T, g.T
    dqt_parts, att_parts, dk_parts, dv_parts = [], [], [], []
    for patch in range(patches):
        here = slice(patch * frames, (patch + 1) * frames)
        dqt_p, att_p, dk_p, dv_p = [], [], [], []
        for pair in range(HEADS // 2):
            lanes = slice(pair * 2 * hw, (pair + 1) * 2 * hw)
            p = softmax_rows(mm(k[here, lanes], both_heads(qt[lanes, here], hw, 0, 1)))
            dp = mm(v[here, lanes], both_heads(gt[lanes, here], hw, 0, 1))
            ds = score_back(p, dp)
            for sub in range(2):
                own = slice((2 * pair + sub) * hw, (2 * pair + sub + 1) * hw)
                cols = slice(sub * frames, (sub + 1) * frames)
                att_p.append(mm(vt[own, here], p[:, cols]).astype(B16))
                dqt_p.append((mm(kt[own, here], ds[:, cols]) * (hw ** -0.5)).astype(B16))
            dk_p.append(mm(ds, both_heads(q[here, lanes], hw, 1, 0)).astype(B16))
            dv_p.append(mm(p, both_heads(g[here, lanes], hw, 1, 0)).astype(B16))
        dqt_parts.append(jnp.concatenate(dqt_p, 0))
        att_parts.append(jnp.concatenate(att_p, 0))
        dk_parts.append(jnp.concatenate(dk_p, 1))
        dv_parts.append(jnp.concatenate(dv_p, 1))
    dqt = jnp.concatenate(dqt_parts, 1)
    att_ref[...] = jnp.concatenate(att_parts, 1).T
    dk = jnp.concatenate(dk_parts, 0)
    dv = jnp.concatenate(dv_parts, 0)
    dct_ref[:width] = dqt
    dct_ref[width : 2 * width] = dk.T
    dct_ref[2 * width :] = dv.T
    u = (
        mm(dqt.T, w_ref[:, :width], NT)
        + mm(dk, w_ref[:, width : 2 * width], NT)
        + mm(dv, w_ref[:, 2 * width :], NT)
    )
    branch = normalize_back(scaled, inverse, u).astype(B16)
    scatter = regroup(rows, patches, frames)
    branch_ref[...] = mm(scatter, branch).astype(B16).reshape(branch_ref.shape)


def temporal(st, ct, w, wo):
    frames, patches, width = st.shape
    rows = frames * patches
    return pl.pallas_call(
        temporal_kernel,
        out_shape=(
            jax.ShapeDtypeStruct(st.shape, B16),
            jax.ShapeDtypeStruct((rows, width), B16),
            jax.ShapeDtypeStruct((rows, width), B16),
            jax.ShapeDtypeStruct((rows, width), B16),
            jax.ShapeDtypeStruct((3 * width, rows), B16),
        ),
        in_specs=[VM] * 4,
        out_specs=(VM,) * 5,
        compiler_params=pltpu.CompilerParams(vmem_limit_bytes=16 << 20),
        cost_estimate=pl.CostEstimate(flops=3_000_000_000, bytes_accessed=5_000_000, transcendentals=400_000),
        name="temporal",
    )(st, ct, w, wo)


def spread(slab_ref, onehot_ref, gq, go):
    groups = slab_ref.shape[1]
    a, b = gq.shape[0] // groups, go.shape[0] // groups
    for x in range(groups):
        source = jnp.concatenate([gq[x * a : (x + 1) * a], go[x * b : (x + 1) * b]], 0)
        moved = mm(onehot_ref[...], source).astype(B16)
        slab_ref[:, x] = moved.reshape(slab_ref.shape[:1] + slab_ref.shape[2:])


def weight_kernel(factor, normed_ref, cot_ref, att_ref, dct_ref, onehot_ref, slab_ref):
    gq = (mm(dct_ref[...], normed_ref[...]) * factor).astype(B16)
    go = (mm(cot_ref[...].T, att_ref[...]) * factor).astype(B16)
    spread(slab_ref, onehot_ref, gq, go)


def weight_slabs(factor, normed, cot, att, dct, onehot, shape):
    return pl.pallas_call(
        functools.partial(weight_kernel, factor),
        out_shape=jax.ShapeDtypeStruct(shape, B16),
        in_specs=[VM] * 5,
        out_specs=VM,
        compiler_params=pltpu.CompilerParams(vmem_limit_bytes=16 << 20),
        cost_estimate=pl.CostEstimate(flops=1_500_000_000, bytes_accessed=4_000_000, transcendentals=0),
        name="weight_slabs",
    )(normed, cot, att, dct, onehot)


def spatial_backward_kernel(
    factor, tok_ref, ct_ref, br_ref, comb_ref, att_ref, probs_ref, wo_ref, onehot_ref,
    slab_ref, sg_ref, dcomb_ref,
):
    rows, width = tok_ref.shape
    hw = width // HEADS
    branch = br_ref[...].reshape(rows, width)
    sg = (ct_ref[...].astype(F32) + branch.astype(F32)).astype(B16)
    sg_ref[...] = sg
    g = mm(sg, wo_ref[...], NT).astype(B16)
    gt = g.T
    q = comb_ref[:, :width] * (hw ** -0.5)
    kt = comb_ref[:, width : 2 * width].T
    dqt_parts, dk_parts, dv_parts = [], [], []
    for pair in range(HEADS // 2):
        lanes = slice(pair * 2 * hw, (pair + 1) * 2 * hw)
        values = comb_ref[:, 2 * width + pair * 2 * hw : 2 * width + (pair + 1) * 2 * hw]
        dk = dv = 0.0
        for sub in range(2):
            head = 2 * pair + sub
            p = probs_ref[head]
            ds = score_back(p, mm(values, one_head(gt[lanes], sub, hw, 0)))
            dqt = mm(kt[head * hw : (head + 1) * hw], ds) * (hw ** -0.5)
            dqt_parts.append(dqt.astype(B16))
            dk = dk + mm(ds, one_head(q[:, lanes], sub, hw, 1))
            dv = dv + mm(p, one_head(g[:, lanes], sub, hw, 1))
        dk_parts.append(dk.astype(B16))
        dv_parts.append(dv.astype(B16))
    dqt = jnp.concatenate(dqt_parts, 0)
    dk = jnp.concatenate(dk_parts, 1)
    dv = jnp.concatenate(dv_parts, 1)
    dcomb_ref[:, :width] = dqt.T
    dcomb_ref[:, width : 2 * width] = dk
    dcomb_ref[:, 2 * width :] = dv
    scaled, _ = normalize(tok_ref[...].astype(F32))
    normed = scaled.astype(B16)
    dct = jnp.concatenate([dqt, dk.T, dv.T], 0)
    gq = (mm(dct, normed) * factor).astype(B16)
    go = (mm(sg.T, att_ref[...]) * factor).astype(B16)
    spread(slab_ref, onehot_ref, gq, go)


def spatial_backward(factor, tokens, ct, branch, comb, att, probs, wo, onehot, shape):
    rows, width = tokens.shape
    return pl.pallas_call(
        functools.partial(spatial_backward_kernel, factor),
        out_shape=(
            jax.ShapeDtypeStruct(shape, B16),
            jax.ShapeDtypeStruct((rows, width), B16),
            jax.ShapeDtypeStruct((rows, 3 * width), B16),
        ),
        in_specs=[VM] * 8,
        out_specs=(VM,) * 3,
        compiler_params=pltpu.CompilerParams(vmem_limit_bytes=16 << 20),
        cost_estimate=pl.CostEstimate(flops=4_000_000_000, bytes_accessed=9_000_000, transcendentals=0),
        name="spatial_backward",
    )(tokens, ct, branch, comb, att, probs, wo, onehot)


def token_kernel(tok_ref, sg_ref, dcomb_ref, w_ref, out_ref):
    scaled, inverse = normalize(tok_ref[...].astype(F32))
    u = mm(dcomb_ref[...], w_ref[...], NT)
    out_ref[...] = (sg_ref[...].astype(F32) + normalize_back(scaled, inverse, u)).astype(B16)


def token_gradient(tokens, sg, dcomb, w):
    return pl.pallas_call(
        token_kernel,
        out_shape=jax.ShapeDtypeStruct(tokens.shape, B16),
        in_specs=[VM] * 4,
        out_specs=VM,
        compiler_params=pltpu.CompilerParams(vmem_limit_bytes=16 << 20),
        cost_estimate=pl.CostEstimate(flops=500_000_000, bytes_accessed=3_000_000, transcendentals=0),
        name="token_gradient",
    )(tokens, sg, dcomb, w)


SEQ = (("x", 4), ("yh", 2), ("z", 8), ("core", 2))


def seq_size():
    return lax.axis_size("seq")


def place(name):
    stride = 1
    for member, size in reversed(SEQ):
        if member == name:
            return stride, size
        stride *= size


def coordinate(name):
    stride, size = place(name)
    return lax.axis_index("seq") // stride % size


def shift(array, name, step):
    stride, size = place(name)
    pairs = []
    for index in range(seq_size()):
        at = index // stride % size
        pairs.append((index, index + ((at + step) % size - at) * stride))
    return lax.ppermute(array, "seq", pairs)


def stage(chunks, name):
    size = chunks.shape[0]
    here = coordinate(name)
    total = lax.dynamic_index_in_dim(chunks, here, 0, keepdims=False).astype(jnp.float32)
    for step in range(1, size):
        part = lax.dynamic_index_in_dim(chunks, (here + step) % size, 0, keepdims=False)
        total = total + shift(part, name, step).astype(jnp.float32)
    return total


def slab_order(width):
    sizes = dict(SEQ)
    a, b = 3 * width // seq_size(), width // seq_size()
    group = seq_size() // sizes["x"]
    table = np.zeros(((a + b) * group, (a + b) * group), np.float32)
    row = 0
    for core in range(sizes["core"]):
        for z in range(sizes["z"]):
            for yh in range(sizes["yh"]):
                member = (yh * sizes["z"] + z) * sizes["core"] + core
                for i in range(a + b):
                    source = member * a + i if i < a else group * a + member * b + i - a
                    table[row, source] = 1.0
                    row += 1
    shape = (sizes["core"], sizes["x"], sizes["z"], sizes["yh"] * (a + b), width)
    return jnp.asarray(table, B16), shape


def first_stages(slabs):
    part = stage(slabs, "core").astype(B16)
    return stage(part, "x").astype(B16)


def last_stages(part):
    part = stage(part, "z").astype(B16)
    part = stage(part, "yh").astype(B16)
    other = lax.ppermute(part, "dp", [(0, 1), (1, 0)])
    return part.astype(F32) + other.astype(F32)


def on_device(tokens, cotangent, wqkv_spatial, wo_spatial, wqkv_temporal, wo_temporal):
    clips, frames, patches, width = tokens.shape
    factor = (clips * frames * patches * lax.axis_size("dp") * seq_size()) ** (-0.5)
    table, slab_shape = slab_order(width)
    tok = tokens.reshape(patches, width)
    cot = cotangent.reshape(patches, width)
    traded = (seq_size(), patches // seq_size(), width)

    def trade(array):
        return lax.all_to_all(array, "seq", split_axis=0, concat_axis=0, tiled=True)

    cot_t = trade(cot.reshape(traded))
    stream, comb, att, probs = spatial_forward(tok, wqkv_spatial, wo_spatial, traded)
    stream, cot_t = lax.optimization_barrier((stream, cot_t))
    stream_t = trade(stream)
    branch, normed_t, cot_p, att_t, dct = temporal(stream_t, cot_t, wqkv_temporal, wo_temporal)
    branch = trade(branch)
    slabs_t = weight_slabs(factor, normed_t, cot_p, att_t, dct, table, slab_shape)
    slabs_s, stream_grad, dcomb = spatial_backward(
        factor, tok, cot, branch, comb, att, probs, wo_spatial, table, slab_shape
    )
    token_grad = token_gradient(tok, stream_grad, dcomb, wqkv_spatial)
    half_t = first_stages(slabs_t)
    half_s = first_stages(slabs_s)
    z, rows = half_s.shape[:2]
    joined = jnp.concatenate(
        [half.reshape(z, 2, rows // 2, width) for half in (half_s, half_t)], 2
    )
    own = last_stages(joined)
    a, b = 3 * width // seq_size(), width // seq_size()
    shares = (own[:a].T, own[a : a + b].T, own[a + b : 2 * a + b].T, own[2 * a + b :].T)
    return (token_grad.reshape(tokens.shape), *shares)


def solution(mesh):
    in_specs = (P("dp", "seq", None, None), P("dp", "seq", None, None), P(), P(), P(), P())
    out_specs = (
        P("dp", "seq", None, None),
        P(None, "seq"),
        P(None, "seq"),
        P(None, "seq"),
        P(None, "seq"),
    )
    return jax.shard_map(
        on_device, mesh=mesh, in_specs=in_specs, out_specs=out_specs, check_vma=False
    )
```

```python
import functools

import jax
import jax.numpy as jnp
import numpy as np
from jax import lax
from jax.experimental import pallas as pl
from jax.experimental.pallas import tpu as pltpu
from jax.sharding import PartitionSpec as P

HEADS = 6
F32 = jnp.float32
B16 = jnp.bfloat16
NN = (((1,), (0,)), ((), ()))
NT = (((1,), (1,)), ((), ()))
VM = pl.BlockSpec(memory_space=pltpu.VMEM)


def mm(left, right, dims=NN):
    return lax.dot_general(left, right, dims, preferred_element_type=F32)


def normalize(values):
    average = jnp.mean(values, -1, keepdims=True)
    centered = values - average
    spread = jnp.mean(centered * centered, -1, keepdims=True)
    inverse = lax.rsqrt(spread + 1e-06)
    return centered * inverse, inverse


def normalize_back(scaled, inverse, upstream):
    return inverse * (
        upstream
        - jnp.mean(upstream, -1, keepdims=True)
        - scaled * jnp.mean(upstream * scaled, -1, keepdims=True)
    )


def one_head(block, sub, half, rows_axis):
    at = lax.broadcasted_iota(jnp.int32, block.shape, rows_axis)
    keep = (at < half) if sub == 0 else (at >= half)
    return jnp.where(keep, block, jnp.zeros_like(block))


def softmax_rows(scores):
    e = jnp.exp(scores - jnp.max(scores, 0, keepdims=True))
    return (e * (1.0 / jnp.sum(e, 0, keepdims=True))).astype(B16)


def score_back(probs, prob_grad):
    weights = probs.astype(F32)
    total = jnp.sum(weights * prob_grad, 0, keepdims=True)
    return (weights * (prob_grad - total)).astype(B16)


def both_heads(block, half, rows_axis, join_axis):
    return jnp.concatenate(
        [one_head(block, 0, half, rows_axis), one_head(block, 1, half, rows_axis)], join_axis
    )


def regroup(count, inner, outer):
    row = lax.broadcasted_iota(jnp.int32, (count, count), 0)
    column = lax.broadcasted_iota(jnp.int32, (count, count), 1)
    source = (row & (inner - 1)) * outer + lax.shift_right_logical(row, inner.bit_length() - 1)
    return (column == source).astype(F32).astype(B16)


HBM = pl.BlockSpec(memory_space=pltpu.HBM)


def call(kernel, arrays, outs, in_specs, out_specs, scratch, copies, flops, exps=0):
    return pl.pallas_call(
        kernel,
        out_shape=tuple(jax.ShapeDtypeStruct(shape, B16) for shape in outs),
        in_specs=in_specs,
        out_specs=tuple(out_specs),
        scratch_shapes=[pltpu.VMEM(shape, B16) for shape in scratch]
        + [pltpu.SemaphoreType.DMA((copies,))],
        cost_estimate=pl.CostEstimate(
            flops=flops,
            bytes_accessed=sum(array.size * 2 for array in arrays),
            transcendentals=exps,
        ),
    )(*arrays)


class Copies:
    def __init__(self, sems):
        self.sems, self.pending = sems, []

    def start(self, source, target):
        copy = pltpu.make_async_copy(source, target, self.sems.at[len(self.pending)])
        self.pending.append(copy)
        copy.start()
        return copy


def spatial_forward_kernel(
    tok_hbm, cot_hbm, w_hbm, wo_hbm, slab_ref, comb_hbm, att_hbm, probs_hbm,
    tok_ref, cot_ref, w_ref, wo_ref, comb_ref, att_ref, probs_ref, sems,
):
    copies = Copies(sems)
    tok_in = copies.start(tok_hbm, tok_ref)
    w_in = copies.start(w_hbm, w_ref)
    wo_in = copies.start(wo_hbm, wo_ref)
    cot_in = copies.start(cot_hbm, cot_ref)
    width = tok_ref.shape[-1]
    hw = width // HEADS
    outs = []
    tok_in.wait()
    x = tok_ref[...].astype(F32)
    scaled, _ = normalize(x)
    w_in.wait()
    comb = mm(scaled.astype(B16), w_ref[...]).astype(B16)
    comb_ref[...] = comb
    outs.append(copies.start(comb_ref, comb_hbm))
    qt = (comb[:, :width] * (hw ** -0.5)).T
    vt = comb[:, 2 * width :].T
    parts = []
    for pair in range(HEADS // 2):
        at = pair * 2 * hw
        keys = comb[:, width + at : width + at + 2 * hw]
        for sub in range(2):
            head = 2 * pair + sub
            p = softmax_rows(mm(keys, one_head(qt[at : at + 2 * hw], sub, hw, 0)))
            probs_ref[head] = p
            outs.append(copies.start(probs_ref.at[head], probs_hbm.at[head]))
            parts.append(mm(vt[head * hw : (head + 1) * hw], p).astype(B16))
    att = jnp.concatenate(parts, 0).T
    att_ref[...] = att
    outs.append(copies.start(att_ref, att_hbm))
    wo_in.wait()
    out = (x + mm(att, wo_ref[...])).astype(B16)
    cot_in.wait()
    half = (slab_ref.shape[0], slab_ref.shape[1] // 2, width)
    slab_ref[...] = jnp.concatenate([out.reshape(half), cot_ref[...].reshape(half)], 1)
    for copy in outs:
        copy.wait()


def spatial_forward(tokens, cotangent, w, wo, slab):
    rows, width = tokens.shape
    wide, square = (rows, 3 * width), (rows, width)
    probs = (HEADS, rows, rows)
    return call(
        spatial_forward_kernel, (tokens, cotangent, w, wo),
        (slab, wide, square, probs), [HBM] * 4, [VM] + [HBM] * 3,
        [square, square, w.shape, wo.shape, wide, square, probs],
        6 + HEADS, 2_000_000_000, 1_600_000,
    )


def temporal_kernel(
    slab_ref, w_hbm, wo_hbm, branch_ref, normed_hbm, cot_hbm, att_hbm, dct_hbm,
    w_ref, wo_ref, normed_ref, cot_ref, att_ref, dct_ref, sems,
):
    copies = Copies(sems)
    w_in = copies.start(w_hbm, w_ref)
    wo_in = copies.start(wo_hbm, wo_ref)
    frames, both, width = slab_ref.shape
    patches = both // 2
    rows = frames * patches
    hw = width // HEADS
    gather = regroup(rows, frames, patches)
    slab = slab_ref[...]
    x = mm(gather, slab[:, :patches].reshape(rows, width))
    cot = mm(gather, slab[:, patches:].reshape(rows, width)).astype(B16)
    cot_ref[...] = cot
    outs = [copies.start(cot_ref, cot_hbm)]
    scaled, inverse = normalize(x)
    normed = scaled.astype(B16)
    normed_ref[...] = normed
    outs.append(copies.start(normed_ref, normed_hbm))
    w_in.wait()
    comb = mm(normed, w_ref[...]).astype(B16)
    wo_in.wait()
    g = mm(cot, wo_ref[...], NT).astype(B16)
    q = comb[:, :width] * (hw ** -0.5)
    k = comb[:, width : 2 * width]
    v = comb[:, 2 * width :]
    qt, kt, vt, gt = q.T, k.T, v.T, g.T
    dqt_parts, att_parts, dk_parts, dv_parts = [], [], [], []
    for patch in range(patches):
        here = slice(patch * frames, (patch + 1) * frames)
        dqt_p, att_p, dk_p, dv_p = [], [], [], []
        for pair in range(HEADS // 2):
            lanes = slice(pair * 2 * hw, (pair + 1) * 2 * hw)
            p = softmax_rows(mm(k[here, lanes], both_heads(qt[lanes, here], hw, 0, 1)))
            dp = mm(v[here, lanes], both_heads(gt[lanes, here], hw, 0, 1))
            ds = score_back(p, dp)
            for sub in range(2):
                own = slice((2 * pair + sub) * hw, (2 * pair + sub + 1) * hw)
                cols = slice(sub * frames, (sub + 1) * frames)
                att_p.append(mm(vt[own, here], p[:, cols]).astype(B16))
                dqt_p.append((mm(kt[own, here], ds[:, cols]) * (hw ** -0.5)).astype(B16))
            dk_p.append(mm(ds, both_heads(q[here, lanes], hw, 1, 0)).astype(B16))
            dv_p.append(mm(p, both_heads(g[here, lanes], hw, 1, 0)).astype(B16))
        dqt_parts.append(jnp.concatenate(dqt_p, 0))
        att_parts.append(jnp.concatenate(att_p, 0))
        dk_parts.append(jnp.concatenate(dk_p, 1))
        dv_parts.append(jnp.concatenate(dv_p, 1))
    dqt = jnp.concatenate(dqt_parts, 1)
    att_ref[...] = jnp.concatenate(att_parts, 1).T
    outs.append(copies.start(att_ref, att_hbm))
    dk = jnp.concatenate(dk_parts, 0)
    dv = jnp.concatenate(dv_parts, 0)
    dct_ref[:width] = dqt
    dct_ref[width : 2 * width] = dk.T
    dct_ref[2 * width :] = dv.T
    outs.append(copies.start(dct_ref, dct_hbm))
    u = (
        mm(dqt.T, w_ref[:, :width], NT)
        + mm(dk, w_ref[:, width : 2 * width], NT)
        + mm(dv, w_ref[:, 2 * width :], NT)
    )
    branch = normalize_back(scaled, inverse, u).astype(B16)
    scatter = regroup(rows, patches, frames)
    branch_ref[...] = mm(scatter, branch).astype(B16).reshape(branch_ref.shape)
    for copy in outs:
        copy.wait()


def temporal(slab, w, wo):
    frames, both, width = slab.shape
    rows = frames * both // 2
    square = (rows, width)
    return call(
        temporal_kernel, (slab, w, wo),
        ((frames, both // 2, width), square, square, square, (3 * width, rows)),
        [VM, HBM, HBM], [VM] + [HBM] * 4,
        [w.shape, wo.shape, square, square, square, (3 * width, rows)],
        6, 3_000_000_000, 400_000,
    )


def spread(copies, onehot, gq, go, slab_ref, own_hbm, send_hbm):
    here = lax.axis_index("seq") % slab_ref.shape[0]
    groups = slab_ref.shape[1]
    a, b = gq.shape[0] // groups, go.shape[0] // groups
    outs = []
    for x in range(groups):
        source = jnp.concatenate([gq[x * a : (x + 1) * a], go[x * b : (x + 1) * b]], 0)
        moved = mm(onehot, source).astype(B16)
        slab_ref[:, x] = moved.reshape(slab_ref.shape[:1] + slab_ref.shape[2:])
        outs.append(copies.start(slab_ref.at[1 - here, x], send_hbm.at[x]))
        outs.append(copies.start(slab_ref.at[here, x], own_hbm.at[x]))
    return outs


def weight_kernel(
    factor, normed_hbm, cot_hbm, att_hbm, dct_hbm, onehot_hbm, own_hbm, send_hbm,
    normed_ref, cot_ref, att_ref, dct_ref, onehot_ref, slab_ref, sems,
):
    copies = Copies(sems)
    cot_in = copies.start(cot_hbm, cot_ref)
    att_in = copies.start(att_hbm, att_ref)
    normed_in = copies.start(normed_hbm, normed_ref)
    dct_in = copies.start(dct_hbm, dct_ref)
    onehot_in = copies.start(onehot_hbm, onehot_ref)
    cot_in.wait()
    att_in.wait()
    go = (mm(cot_ref[...].T, att_ref[...]) * factor).astype(B16)
    normed_in.wait()
    dct_in.wait()
    gq = (mm(dct_ref[...], normed_ref[...]) * factor).astype(B16)
    onehot_in.wait()
    for copy in spread(copies, onehot_ref[...], gq, go, slab_ref, own_hbm, send_hbm):
        copy.wait()


def weight_slabs(factor, normed, cot, att, dct, onehot, shape):
    arrays = (normed, cot, att, dct, onehot)
    return call(
        functools.partial(weight_kernel, factor), arrays,
        (shape[1:], shape[1:]), [HBM] * 5, [HBM] * 2,
        [array.shape for array in arrays] + [shape], 5 + 2 * shape[1], 1_500_000_000,
    )


def spatial_backward_kernel(
    factor, ct_hbm, br_hbm, wo_hbm, comb_hbm, probs_hbm, tok_hbm, att_hbm, onehot_hbm,
    own_hbm, send_hbm, sg_hbm, dcomb_hbm,
    ct_ref, br_ref, wo_ref, comb_ref, probs_ref, tok_ref, att_ref, onehot_ref,
    slab_ref, sg_ref, dcomb_ref, sems,
):
    copies = Copies(sems)
    br_in = copies.start(br_hbm, br_ref)
    ct_in = copies.start(ct_hbm, ct_ref)
    wo_in = copies.start(wo_hbm, wo_ref)
    comb_in = copies.start(comb_hbm, comb_ref)
    probs_in = [copies.start(probs_hbm.at[h], probs_ref.at[h]) for h in range(HEADS)]
    tok_in = copies.start(tok_hbm, tok_ref)
    att_in = copies.start(att_hbm, att_ref)
    onehot_in = copies.start(onehot_hbm, onehot_ref)
    rows, width = ct_ref.shape
    hw = width // HEADS
    br_in.wait()
    ct_in.wait()
    branch = br_ref[...].reshape(rows, width)
    sg = (ct_ref[...].astype(F32) + branch.astype(F32)).astype(B16)
    sg_ref[...] = sg
    outs = [copies.start(sg_ref, sg_hbm)]
    wo_in.wait()
    g = mm(sg, wo_ref[...], NT).astype(B16)
    gt = g.T
    comb_in.wait()
    q = comb_ref[:, :width] * (hw ** -0.5)
    kt = comb_ref[:, width : 2 * width].T
    dqt_parts, dk_parts, dv_parts = [], [], []
    for pair in range(HEADS // 2):
        lanes = slice(pair * 2 * hw, (pair + 1) * 2 * hw)
        values = comb_ref[:, 2 * width + pair * 2 * hw : 2 * width + (pair + 1) * 2 * hw]
        dk = dv = 0.0
        for sub in range(2):
            head = 2 * pair + sub
            probs_in[head].wait()
            p = probs_ref[head]
            ds = score_back(p, mm(values, one_head(gt[lanes], sub, hw, 0)))
            dqt = mm(kt[head * hw : (head + 1) * hw], ds) * (hw ** -0.5)
            dqt_parts.append(dqt.astype(B16))
            dk = dk + mm(ds, one_head(q[:, lanes], sub, hw, 1))
            dv = dv + mm(p, one_head(g[:, lanes], sub, hw, 1))
        dk_parts.append(dk.astype(B16))
        dv_parts.append(dv.astype(B16))
    dqt = jnp.concatenate(dqt_parts, 0)
    dk = jnp.concatenate(dk_parts, 1)
    dv = jnp.concatenate(dv_parts, 1)
    tok_in.wait()
    scaled, _ = normalize(tok_ref[...].astype(F32))
    normed = scaled.astype(B16)
    dct = jnp.concatenate([dqt, dk.T, dv.T], 0)
    gq = (mm(dct, normed) * factor).astype(B16)
    att_in.wait()
    go = (mm(sg.T, att_ref[...]) * factor).astype(B16)
    onehot_in.wait()
    outs += spread(copies, onehot_ref[...], gq, go, slab_ref, own_hbm, send_hbm)
    dcomb_ref[:, :width] = dqt.T
    dcomb_ref[:, width : 2 * width] = dk
    dcomb_ref[:, 2 * width :] = dv
    outs.append(copies.start(dcomb_ref, dcomb_hbm))
    for copy in outs:
        copy.wait()


def spatial_backward(factor, ct, branch, wo, comb, probs, tokens, att, onehot, shape):
    rows, width = tokens.shape
    arrays = (ct, branch, wo, comb, probs, tokens, att, onehot)
    square, wide = (rows, width), (rows, 3 * width)
    return call(
        functools.partial(spatial_backward_kernel, factor), arrays,
        (shape[1:], shape[1:], square, wide), [HBM] * 8, [HBM] * 4,
        [array.shape for array in arrays] + [shape, square, wide],
        9 + HEADS + 2 * shape[1], 4_000_000_000,
    )


def token_kernel(
    tok_hbm, w_hbm, dcomb_hbm, sg_hbm, out_ref, tok_ref, w_ref, dcomb_ref, sg_ref, sems
):
    copies = Copies(sems)
    pending = [
        copies.start(source, target)
        for source, target in (
            (w_hbm, w_ref), (dcomb_hbm, dcomb_ref), (tok_hbm, tok_ref), (sg_hbm, sg_ref)
        )
    ]
    for copy in pending:
        copy.wait()
    scaled, inverse = normalize(tok_ref[...].astype(F32))
    u = mm(dcomb_ref[...], w_ref[...], NT)
    out_ref[...] = (sg_ref[...].astype(F32) + normalize_back(scaled, inverse, u)).astype(B16)


def token_gradient(tokens, w, dcomb, sg):
    arrays = (tokens, w, dcomb, sg)
    return call(
        token_kernel, arrays, (tokens.shape,), [HBM] * 4, [VM],
        [array.shape for array in arrays], 4, 500_000_000,
    )[0]


SEQ = (("x", 4), ("yh", 2), ("z", 8), ("core", 2))


def seq_size():
    return lax.axis_size("seq")


def place(name):
    stride = 1
    for member, size in reversed(SEQ):
        if member == name:
            return stride, size
        stride *= size


def coordinate(name):
    stride, size = place(name)
    return lax.axis_index("seq") // stride % size


def shift(array, name, step):
    stride, size = place(name)
    pairs = []
    for index in range(seq_size()):
        at = index // stride % size
        pairs.append((index, index + ((at + step) % size - at) * stride))
    return lax.ppermute(array, "seq", pairs)


def stage(chunks, name):
    size = chunks.shape[0]
    here = coordinate(name)
    total = lax.dynamic_index_in_dim(chunks, here, 0, keepdims=False).astype(F32)
    for step in range(1, size):
        part = lax.dynamic_index_in_dim(chunks, (here + step) % size, 0, keepdims=False)
        total = total + shift(part, name, step).astype(F32)
    return total


def slab_order(width):
    sizes = dict(SEQ)
    a, b = 3 * width // seq_size(), width // seq_size()
    group = seq_size() // sizes["x"]
    table = np.zeros(((a + b) * group, (a + b) * group), np.float32)
    row = 0
    for core in range(sizes["core"]):
        for z in range(sizes["z"]):
            for yh in range(sizes["yh"]):
                member = (yh * sizes["z"] + z) * sizes["core"] + core
                for i in range(a + b):
                    source = member * a + i if i < a else group * a + member * b + i - a
                    table[row, source] = 1.0
                    row += 1
    shape = (sizes["core"], sizes["x"], sizes["z"], sizes["yh"] * (a + b), width)
    return jnp.asarray(table, B16), shape


def first_stages(own, send):
    part = (own.astype(F32) + shift(send, "core", 1).astype(F32)).astype(B16)
    return stage(part, "x").astype(B16)


def groups_of(*names):
    wanted = [place(name) for name in names]
    groups = []
    for index in range(seq_size()):
        if all(index // stride % size == 0 for stride, size in wanted):
            members = [index]
            for stride, size in wanted:
                members = [at + k * stride for at in members for k in range(size)]
            groups.append(members)
    return groups


def last_stages(part):
    yh, z = part.shape[:2]
    flat = part.reshape(yh * z, *part.shape[2:])
    got = lax.all_to_all(
        flat, "seq", split_axis=0, concat_axis=0, tiled=True, axis_index_groups=groups_of("yh", "z")
    )
    mine = jnp.sum(got.astype(F32), 0).astype(B16)
    other = lax.ppermute(mine, "dp", [(0, 1), (1, 0)])
    return mine.astype(F32) + other.astype(F32)


def on_device(tokens, cotangent, wqkv_spatial, wo_spatial, wqkv_temporal, wo_temporal):
    clips, frames, patches, width = tokens.shape
    factor = (clips * frames * patches * lax.axis_size("dp") * seq_size()) ** (-0.5)
    table, slab_shape = slab_order(width)
    tok = tokens.reshape(patches, width)
    cot = cotangent.reshape(patches, width)
    traded = (seq_size(), 2 * patches // seq_size(), width)

    def trade(array):
        return lax.all_to_all(array, "seq", split_axis=0, concat_axis=0, tiled=True)

    stream, comb, att, probs = spatial_forward(tok, cot, wqkv_spatial, wo_spatial, traded)
    branch, normed_t, cot_p, att_t, dct = temporal(trade(stream), wqkv_temporal, wo_temporal)
    branch = trade(branch)
    own, send = weight_slabs(factor, normed_t, cot_p, att_t, dct, table, slab_shape)
    half_t = first_stages(own, send)
    branch, half_t = lax.optimization_barrier((branch, half_t))
    own, send, stream_grad, dcomb = spatial_backward(
        factor, cot, branch, wo_spatial, comb, probs, tok, att, table, slab_shape
    )
    half_s = first_stages(own, send)
    token_grad = token_gradient(tok, wqkv_spatial, dcomb, stream_grad)
    z, rows = half_s.shape[:2]
    joined = jnp.concatenate(
        [
            jnp.moveaxis(half.reshape(z, 2, rows // 2, width), 1, 0)
            for half in (half_s, half_t)
        ],
        2,
    )
    own = last_stages(joined)
    a, b = 3 * width // seq_size(), width // seq_size()
    shares = (own[:a].T, own[a : a + b].T, own[a + b : 2 * a + b].T, own[2 * a + b :].T)
    return (token_grad.reshape(tokens.shape), *shares)


def solution(mesh):
    in_specs = (P("dp", "seq", None, None), P("dp", "seq", None, None), P(), P(), P(), P())
    out_specs = (
        P("dp", "seq", None, None),
        P(None, "seq"),
        P(None, "seq"),
        P(None, "seq"),
        P(None, "seq"),
    )
    return jax.shard_map(
        on_device, mesh=mesh, in_specs=in_specs, out_specs=out_specs, check_vma=False
    )
```

```python
import functools

import jax
import jax.numpy as jnp
import numpy as np
from jax import lax
from jax.experimental import pallas as pl
from jax.experimental.pallas import tpu as pltpu
from jax.sharding import PartitionSpec as P

HEADS = 6
F32 = jnp.float32
B16 = jnp.bfloat16
NN = (((1,), (0,)), ((), ()))
NT = (((1,), (1,)), ((), ()))
VM = pl.BlockSpec(memory_space=pltpu.VMEM)


def mm(left, right, dims=NN):
    return lax.dot_general(left, right, dims, preferred_element_type=F32)


def normalize(values):
    average = jnp.mean(values, -1, keepdims=True)
    centered = values - average
    spread = jnp.mean(centered * centered, -1, keepdims=True)
    inverse = lax.rsqrt(spread + 1e-06)
    return centered * inverse, inverse


def normalize_back(scaled, inverse, upstream):
    return inverse * (
        upstream
        - jnp.mean(upstream, -1, keepdims=True)
        - scaled * jnp.mean(upstream * scaled, -1, keepdims=True)
    )


def one_head(block, sub, half, rows_axis):
    at = lax.broadcasted_iota(jnp.int32, block.shape, rows_axis)
    keep = (at < half) if sub == 0 else (at >= half)
    return jnp.where(keep, block, jnp.zeros_like(block))


def softmax_rows(scores):
    e = jnp.exp(scores - jnp.max(scores, 0, keepdims=True))
    return (e * (1.0 / jnp.sum(e, 0, keepdims=True))).astype(B16)


def score_back(probs, prob_grad):
    weights = probs.astype(F32)
    total = jnp.sum(weights * prob_grad, 0, keepdims=True)
    return (weights * (prob_grad - total)).astype(B16)


def both_heads(block, half, rows_axis, join_axis):
    return jnp.concatenate(
        [one_head(block, 0, half, rows_axis), one_head(block, 1, half, rows_axis)], join_axis
    )


def regroup(count, inner, outer):
    row = lax.broadcasted_iota(jnp.int32, (count, count), 0)
    column = lax.broadcasted_iota(jnp.int32, (count, count), 1)
    source = (row & (inner - 1)) * outer + lax.shift_right_logical(row, inner.bit_length() - 1)
    return (column == source).astype(F32).astype(B16)


HBM = pl.BlockSpec(memory_space=pltpu.HBM)


def call(kernel, arrays, outs, in_specs, out_specs, scratch, copies, flops, exps=0, limit=None):
    return pl.pallas_call(
        kernel,
        out_shape=tuple(jax.ShapeDtypeStruct(shape, B16) for shape in outs),
        in_specs=in_specs,
        out_specs=tuple(out_specs),
        scratch_shapes=[pltpu.VMEM(shape, B16) for shape in scratch]
        + [pltpu.SemaphoreType.DMA((copies,))],
        compiler_params=pltpu.CompilerParams(vmem_limit_bytes=limit and limit << 20),
        cost_estimate=pl.CostEstimate(
            flops=flops,
            bytes_accessed=sum(array.size * 2 for array in arrays),
            transcendentals=exps,
        ),
    )(*arrays)


class Copies:
    def __init__(self, sems):
        self.sems, self.pending = sems, []

    def start(self, source, target):
        copy = pltpu.make_async_copy(source, target, self.sems.at[len(self.pending)])
        self.pending.append(copy)
        copy.start()
        return copy


def spatial_forward_kernel(
    tok_hbm, cot_hbm, w_hbm, wo_hbm, slab_ref, saved_hbm,
    tok_ref, cot_ref, w_ref, wo_ref, wide_ref, probs_ref, sems,
):
    copies = Copies(sems)
    tok_in = copies.start(tok_hbm, tok_ref)
    w_in = copies.start(w_hbm, w_ref)
    wo_in = copies.start(wo_hbm, wo_ref)
    cot_in = copies.start(cot_hbm, cot_ref)
    width = tok_ref.shape[-1]
    hw = width // HEADS
    outs = []
    tok_in.wait()
    x = tok_ref[...].astype(F32)
    scaled, _ = normalize(x)
    w_in.wait()
    comb = mm(scaled.astype(B16), w_ref[...]).astype(B16)
    wide_ref[:, : 3 * width] = comb
    rows = comb.shape[0]
    for part in range(2):
        outs.append(
            copies.start(wide_ref.at[:, part * rows : (part + 1) * rows], saved_hbm.at[HEADS + part])
        )
    qt = (comb[:, :width] * (hw ** -0.5)).T
    vt = comb[:, 2 * width :].T
    parts = []
    for pair in range(HEADS // 2):
        at = pair * 2 * hw
        keys = comb[:, width + at : width + at + 2 * hw]
        for sub in range(2):
            head = 2 * pair + sub
            p = softmax_rows(mm(keys, one_head(qt[at : at + 2 * hw], sub, hw, 0)))
            probs_ref[head] = p
            outs.append(copies.start(probs_ref.at[head], saved_hbm.at[head]))
            parts.append(mm(vt[head * hw : (head + 1) * hw], p).astype(B16))
    att = jnp.concatenate(parts, 0).T
    wide_ref[:, 3 * width :] = att
    outs.append(copies.start(wide_ref.at[:, 2 * rows :], saved_hbm.at[HEADS + 2]))
    wo_in.wait()
    out = (x + mm(att, wo_ref[...])).astype(B16)
    cot_in.wait()
    half = (slab_ref.shape[0], slab_ref.shape[1] // 2, width)
    slab_ref[...] = jnp.concatenate([out.reshape(half), cot_ref[...].reshape(half)], 1)
    for copy in outs:
        copy.wait()


def spatial_forward(tokens, cotangent, w, wo, slab):
    rows, width = tokens.shape
    wide, square = (rows, 4 * width), (rows, width)
    return call(
        spatial_forward_kernel, (tokens, cotangent, w, wo),
        (slab, (HEADS + 3, rows, rows)), [HBM] * 4, [VM, HBM],
        [square, square, w.shape, wo.shape, wide, (HEADS, rows, rows)],
        7 + HEADS, 2_000_000_000, 1_600_000, None,
    )


def temporal_kernel(
    factor, slab_ref, w_ref, wo_ref, branch_ref, normed_ref, go_ref, dct_ref, _,
):
    frames, both, width = slab_ref.shape
    patches = both // 2
    rows = frames * patches
    hw = width // HEADS
    gather = regroup(rows, frames, patches)
    slab = slab_ref[...]
    x = mm(gather, slab[:, :patches].reshape(rows, width))
    cot = mm(gather, slab[:, patches:].reshape(rows, width)).astype(B16)
    scaled, inverse = normalize(x)
    normed = scaled.astype(B16)
    normed_ref[...] = normed
    comb = mm(normed, w_ref[...]).astype(B16)
    g = mm(cot, wo_ref[...], NT).astype(B16)
    q = comb[:, :width] * (hw ** -0.5)
    k = comb[:, width : 2 * width]
    v = comb[:, 2 * width :]
    qt, kt, vt, gt = q.T, k.T, v.T, g.T
    dqt_parts, att_parts, dk_parts, dv_parts = [], [], [], []
    for patch in range(patches):
        here = slice(patch * frames, (patch + 1) * frames)
        dqt_p, att_p, dk_p, dv_p = [], [], [], []
        for pair in range(HEADS // 2):
            lanes = slice(pair * 2 * hw, (pair + 1) * 2 * hw)
            p = softmax_rows(mm(k[here, lanes], both_heads(qt[lanes, here], hw, 0, 1)))
            dp = mm(v[here, lanes], both_heads(gt[lanes, here], hw, 0, 1))
            ds = score_back(p, dp)
            for sub in range(2):
                own = slice((2 * pair + sub) * hw, (2 * pair + sub + 1) * hw)
                cols = slice(sub * frames, (sub + 1) * frames)
                att_p.append(mm(vt[own, here], p[:, cols]).astype(B16))
                dqt_p.append((mm(kt[own, here], ds[:, cols]) * (hw ** -0.5)).astype(B16))
            dk_p.append(mm(ds, both_heads(q[here, lanes], hw, 1, 0)).astype(B16))
            dv_p.append(mm(p, both_heads(g[here, lanes], hw, 1, 0)).astype(B16))
        dqt_parts.append(jnp.concatenate(dqt_p, 0))
        att_parts.append(jnp.concatenate(att_p, 0))
        dk_parts.append(jnp.concatenate(dk_p, 1))
        dv_parts.append(jnp.concatenate(dv_p, 1))
    dqt = jnp.concatenate(dqt_parts, 1)
    att = jnp.concatenate(att_parts, 1).T
    go_ref[...] = (mm(cot.T, att) * factor).astype(B16)
    dk = jnp.concatenate(dk_parts, 0)
    dv = jnp.concatenate(dv_parts, 0)
    dct_ref[:width] = dqt
    dct_ref[width : 2 * width] = dk.T
    dct_ref[2 * width :] = dv.T
    u = (
        mm(dqt.T, w_ref[:, :width], NT)
        + mm(dk, w_ref[:, width : 2 * width], NT)
        + mm(dv, w_ref[:, 2 * width :], NT)
    )
    branch = normalize_back(scaled, inverse, u).astype(B16)
    scatter = regroup(rows, patches, frames)
    branch_ref[...] = mm(scatter, branch).astype(B16).reshape(branch_ref.shape)


def temporal(factor, slab, w, wo):
    frames, both, width = slab.shape
    rows = frames * both // 2
    return call(
        functools.partial(temporal_kernel, factor), (slab, w, wo),
        ((frames, both // 2, width), (rows, width), wo.shape, (3 * width, rows)),
        [VM] * 3, [VM] * 4, [], 1, 3_000_000_000, 400_000, 48,
    )


def spread(onehot, gq, go, slab_ref, own_ref, send_ref):
    here = lax.axis_index("seq") % slab_ref.shape[0]
    groups = slab_ref.shape[1]
    a, b = gq.shape[0] // groups, go.shape[0] // groups
    for x in range(groups):
        source = jnp.concatenate([gq[x * a : (x + 1) * a], go[x * b : (x + 1) * b]], 0)
        moved = mm(onehot, source).astype(B16)
        slab_ref[:, x] = moved.reshape(slab_ref.shape[:1] + slab_ref.shape[2:])
        send_ref[x] = slab_ref[1 - here, x]
        own_ref[x] = slab_ref[here, x]


def weight_kernel(factor, normed_ref, go_ref, dct_ref, onehot_ref, own_ref, send_ref, slab_ref, _):
    gq = (mm(dct_ref[...], normed_ref[...]) * factor).astype(B16)
    spread(onehot_ref[...], gq, go_ref[...], slab_ref, own_ref, send_ref)


def weight_slabs(factor, normed, go, dct, onehot, shape):
    return call(
        functools.partial(weight_kernel, factor), (normed, go, dct, onehot),
        (shape[1:], shape[1:]), [VM] * 4, [VM] * 2, [shape], 1, 1_500_000_000, 0, 48,
    )


def spatial_backward_kernel(
    factor, ct_ref, br_ref, wo_ref, saved_hbm, tok_ref, onehot_ref,
    own_ref, send_ref, sg_ref, dcomb_ref,
    comb_ref, probs_ref, slab_ref, sems,
):
    copies = Copies(sems)
    rows, width = ct_ref.shape
    comb_in = [
        copies.start(saved_hbm.at[HEADS + part], comb_ref.at[:, part * rows : (part + 1) * rows])
        for part in (2, 0, 1)
    ]
    probs_in = [copies.start(saved_hbm.at[h], probs_ref.at[h]) for h in range(HEADS)]
    hw = width // HEADS
    branch = br_ref[...].reshape(rows, width)
    sg = (ct_ref[...].astype(F32) + branch.astype(F32)).astype(B16)
    sg_ref[...] = sg
    g = mm(sg, wo_ref[...], NT).astype(B16)
    gt = g.T
    scaled, _ = normalize(tok_ref[...].astype(F32))
    normed = scaled.astype(B16)
    for copy in comb_in:
        copy.wait()
    q = comb_ref[:, :width] * (hw ** -0.5)
    kt = comb_ref[:, width : 2 * width].T
    dqt_parts, dk_parts, dv_parts = [], [], []
    for pair in range(HEADS // 2):
        lanes = slice(pair * 2 * hw, (pair + 1) * 2 * hw)
        values = comb_ref[:, 2 * width + pair * 2 * hw : 2 * width + (pair + 1) * 2 * hw]
        dk = dv = 0.0
        for sub in range(2):
            head = 2 * pair + sub
            probs_in[head].wait()
            p = probs_ref[head]
            ds = score_back(p, mm(values, one_head(gt[lanes], sub, hw, 0)))
            dqt = mm(kt[head * hw : (head + 1) * hw], ds) * (hw ** -0.5)
            dqt_parts.append(dqt.astype(B16))
            dk = dk + mm(ds, one_head(q[:, lanes], sub, hw, 1))
            dv = dv + mm(p, one_head(g[:, lanes], sub, hw, 1))
        dk_parts.append(dk.astype(B16))
        dv_parts.append(dv.astype(B16))
    dqt = jnp.concatenate(dqt_parts, 0)
    dk = jnp.concatenate(dk_parts, 1)
    dv = jnp.concatenate(dv_parts, 1)
    dct = jnp.concatenate([dqt, dk.T, dv.T], 0)
    gq = (mm(dct, normed) * factor).astype(B16)
    go = (mm(sg.T, comb_ref[:, 3 * width :]) * factor).astype(B16)
    spread(onehot_ref[...], gq, go, slab_ref, own_ref, send_ref)
    dcomb_ref[:, :width] = dqt.T
    dcomb_ref[:, width : 2 * width] = dk
    dcomb_ref[:, 2 * width :] = dv


def spatial_backward(factor, ct, branch, wo, saved, tokens, onehot, shape):
    rows, width = tokens.shape
    arrays = (ct, branch, wo, saved, tokens, onehot)
    square, wide = (rows, width), (rows, 3 * width)
    return call(
        functools.partial(spatial_backward_kernel, factor), arrays,
        (shape[1:], shape[1:], square, wide),
        [VM, VM, VM, HBM, VM, VM], [VM] * 4,
        [(rows, 4 * width), (HEADS, rows, rows), shape], 3 + HEADS, 4_000_000_000, 0, 48,
    )


def token_kernel(tok_ref, w_ref, dcomb_ref, sg_ref, out_ref, _):
    scaled, inverse = normalize(tok_ref[...].astype(F32))
    u = mm(dcomb_ref[...], w_ref[...], NT)
    out_ref[...] = (sg_ref[...].astype(F32) + normalize_back(scaled, inverse, u)).astype(B16)


def token_gradient(tokens, w, dcomb, sg):
    return call(
        token_kernel, (tokens, w, dcomb, sg), (tokens.shape,),
        [VM] * 4, [VM], [], 1, 500_000_000, 0, 48,
    )[0]


SEQ = (("x", 4), ("yh", 2), ("z", 8), ("core", 2))


def seq_size():
    return lax.axis_size("seq")


def place(name):
    stride = 1
    for member, size in reversed(SEQ):
        if member == name:
            return stride, size
        stride *= size


def coordinate(name):
    stride, size = place(name)
    return lax.axis_index("seq") // stride % size


def shift(array, name, step):
    stride, size = place(name)
    pairs = []
    for index in range(seq_size()):
        at = index // stride % size
        pairs.append((index, index + ((at + step) % size - at) * stride))
    return lax.ppermute(array, "seq", pairs)


def stage(chunks, name):
    size = chunks.shape[0]
    here = coordinate(name)
    total = lax.dynamic_index_in_dim(chunks, here, 0, keepdims=False).astype(F32)
    for step in range(1, size):
        part = lax.dynamic_index_in_dim(chunks, (here + step) % size, 0, keepdims=False)
        total = total + shift(part, name, step).astype(F32)
    return total


def slab_order(width):
    sizes = dict(SEQ)
    a, b = 3 * width // seq_size(), width // seq_size()
    group = seq_size() // sizes["x"]
    table = np.zeros(((a + b) * group, (a + b) * group), np.float32)
    row = 0
    for core in range(sizes["core"]):
        for z in range(sizes["z"]):
            for yh in range(sizes["yh"]):
                member = (yh * sizes["z"] + z) * sizes["core"] + core
                for i in range(a + b):
                    source = member * a + i if i < a else group * a + member * b + i - a
                    table[row, source] = 1.0
                    row += 1
    shape = (sizes["core"], sizes["x"], sizes["z"], sizes["yh"] * (a + b), width)
    return jnp.asarray(table, B16), shape


def first_stages(own, send):
    part = (own.astype(F32) + shift(send, "core", 1).astype(F32)).astype(B16)
    return stage(part, "x").astype(B16)


def groups_of(*names):
    wanted = [place(name) for name in names]
    groups = []
    for index in range(seq_size()):
        if all(index // stride % size == 0 for stride, size in wanted):
            members = [index]
            for stride, size in wanted:
                members = [at + k * stride for at in members for k in range(size)]
            groups.append(members)
    return groups


def last_stages(part):
    yh, z = part.shape[:2]
    flat = part.reshape(yh * z, *part.shape[2:])
    got = lax.all_to_all(
        flat, "seq", split_axis=0, concat_axis=0, tiled=True, axis_index_groups=groups_of("yh", "z")
    )
    mine = jnp.sum(got.astype(F32), 0).astype(B16)
    other = lax.ppermute(mine, "dp", [(0, 1), (1, 0)])
    return mine.astype(F32) + other.astype(F32)


def on_device(tokens, cotangent, wqkv_spatial, wo_spatial, wqkv_temporal, wo_temporal):
    clips, frames, patches, width = tokens.shape
    factor = (clips * frames * patches * lax.axis_size("dp") * seq_size()) ** (-0.5)
    table, slab_shape = slab_order(width)
    tok = tokens.reshape(patches, width)
    cot = cotangent.reshape(patches, width)
    traded = (seq_size(), 2 * patches // seq_size(), width)

    def trade(array):
        return lax.all_to_all(array, "seq", split_axis=0, concat_axis=0, tiled=True)

    stream, saved = spatial_forward(tok, cot, wqkv_spatial, wo_spatial, traded)
    branch, normed_t, go_t, dct = temporal(factor, trade(stream), wqkv_temporal, wo_temporal)
    branch = trade(branch)
    own, send = weight_slabs(factor, normed_t, go_t, dct, table, slab_shape)
    half_t = first_stages(own, send)
    own, send, stream_grad, dcomb = spatial_backward(
        factor, cot, branch, wo_spatial, saved, tok, table, slab_shape
    )
    half_s = first_stages(own, send)
    token_grad = token_gradient(tok, wqkv_spatial, dcomb, stream_grad)
    z, rows = half_s.shape[:2]
    joined = jnp.concatenate(
        [
            jnp.moveaxis(half.reshape(z, 2, rows // 2, width), 1, 0)
            for half in (half_s, half_t)
        ],
        2,
    )
    own = last_stages(joined)
    a, b = 3 * width // seq_size(), width // seq_size()
    shares = (own[:a].T, own[a : a + b].T, own[a + b : 2 * a + b].T, own[2 * a + b :].T)
    return (token_grad.reshape(tokens.shape), *shares)


def solution(mesh):
    in_specs = (P("dp", "seq", None, None), P("dp", "seq", None, None), P(), P(), P(), P())
    out_specs = (
        P("dp", "seq", None, None),
        P(None, "seq"),
        P(None, "seq"),
        P(None, "seq"),
        P(None, "seq"),
    )
    return jax.shard_map(
        on_device, mesh=mesh, in_specs=in_specs, out_specs=out_specs, check_vma=False
    )
```

```python
import functools

import jax
import jax.numpy as jnp
from jax import lax
from jax.experimental import pallas as pl
from jax.experimental.pallas import tpu as pltpu
from jax.sharding import PartitionSpec as P

HEADS = 6
F32 = jnp.float32
B16 = jnp.bfloat16
NN = (((1,), (0,)), ((), ()))
NT = (((1,), (1,)), ((), ()))
VM = pl.BlockSpec(memory_space=pltpu.VMEM)


def mm(left, right, dims=NN):
    return lax.dot_general(left, right, dims, preferred_element_type=F32)


def normalize(values):
    average = jnp.mean(values, -1, keepdims=True)
    centered = values - average
    spread = jnp.mean(centered * centered, -1, keepdims=True)
    inverse = lax.rsqrt(spread + 1e-06)
    return centered * inverse, inverse


def normalize_back(scaled, inverse, upstream):
    return inverse * (
        upstream
        - jnp.mean(upstream, -1, keepdims=True)
        - scaled * jnp.mean(upstream * scaled, -1, keepdims=True)
    )


def one_head(block, sub, half, rows_axis):
    at = lax.broadcasted_iota(jnp.int32, block.shape, rows_axis)
    keep = (at < half) if sub == 0 else (at >= half)
    return jnp.where(keep, block, jnp.zeros_like(block))


def softmax_rows(scores):
    e = jnp.exp(scores - jnp.max(scores, 0, keepdims=True))
    return (e * (1.0 / jnp.sum(e, 0, keepdims=True))).astype(B16)


def score_back(probs, prob_grad):
    weights = probs.astype(F32)
    total = jnp.sum(weights * prob_grad, 0, keepdims=True)
    return (weights * (prob_grad - total)).astype(B16)


def both_heads(block, half, rows_axis, join_axis):
    return jnp.concatenate(
        [one_head(block, 0, half, rows_axis), one_head(block, 1, half, rows_axis)], join_axis
    )


def regroup(count, inner, outer):
    row = lax.broadcasted_iota(jnp.int32, (count, count), 0)
    column = lax.broadcasted_iota(jnp.int32, (count, count), 1)
    source = (row & (inner - 1)) * outer + lax.shift_right_logical(row, inner.bit_length() - 1)
    return (column == source).astype(F32).astype(B16)


HBM = pl.BlockSpec(memory_space=pltpu.HBM)


def call(kernel, arrays, outs, in_specs, out_specs, scratch, copies, flops, exps=0, limit=None):
    return pl.pallas_call(
        kernel,
        out_shape=tuple(jax.ShapeDtypeStruct(shape, B16) for shape in outs),
        in_specs=in_specs,
        out_specs=tuple(out_specs),
        scratch_shapes=[pltpu.VMEM(shape, B16) for shape in scratch]
        + [pltpu.SemaphoreType.DMA((copies,))],
        compiler_params=pltpu.CompilerParams(vmem_limit_bytes=limit and limit << 20),
        cost_estimate=pl.CostEstimate(
            flops=flops,
            bytes_accessed=sum(array.size * 2 for array in arrays),
            transcendentals=exps,
        ),
    )(*arrays)


class Copies:
    def __init__(self, sems):
        self.sems, self.pending = sems, []

    def start(self, source, target):
        copy = pltpu.make_async_copy(source, target, self.sems.at[len(self.pending)])
        self.pending.append(copy)
        copy.start()
        return copy


def spatial_forward_kernel(
    tok_hbm, cot_hbm, w_hbm, wo_hbm, slab_ref, saved_hbm,
    tok_ref, cot_ref, w_ref, wo_ref, wide_ref, probs_ref, sems,
):
    copies = Copies(sems)
    tok_in = copies.start(tok_hbm, tok_ref)
    w_in = copies.start(w_hbm, w_ref)
    wo_in = copies.start(wo_hbm, wo_ref)
    cot_in = copies.start(cot_hbm, cot_ref)
    width = tok_ref.shape[-1]
    hw = width // HEADS
    outs = []
    tok_in.wait()
    x = tok_ref[...].astype(F32)
    scaled, _ = normalize(x)
    w_in.wait()
    comb = mm(scaled.astype(B16), w_ref[...]).astype(B16)
    wide_ref[:, : 3 * width] = comb
    rows = comb.shape[0]
    for part in range(2):
        outs.append(
            copies.start(wide_ref.at[:, part * rows : (part + 1) * rows], saved_hbm.at[HEADS + part])
        )
    qt = (comb[:, :width] * (hw ** -0.5)).T
    vt = comb[:, 2 * width :].T
    parts = []
    for pair in range(HEADS // 2):
        at = pair * 2 * hw
        keys = comb[:, width + at : width + at + 2 * hw]
        for sub in range(2):
            head = 2 * pair + sub
            p = softmax_rows(mm(keys, one_head(qt[at : at + 2 * hw], sub, hw, 0)))
            probs_ref[head] = p
            outs.append(copies.start(probs_ref.at[head], saved_hbm.at[head]))
            parts.append(mm(vt[head * hw : (head + 1) * hw], p).astype(B16))
    att = jnp.concatenate(parts, 0).T
    wide_ref[:, 3 * width :] = att
    outs.append(copies.start(wide_ref.at[:, 2 * rows :], saved_hbm.at[HEADS + 2]))
    wo_in.wait()
    out = (x + mm(att, wo_ref[...])).astype(B16)
    cot_in.wait()
    half = (slab_ref.shape[0],) + slab_ref.shape[2:]
    slab_ref[:, 0] = out.reshape(half)
    slab_ref[:, 1] = cot_ref[...].reshape(half)
    for copy in outs:
        copy.wait()


def spatial_forward(tokens, cotangent, w, wo, slab):
    rows, width = tokens.shape
    wide, square = (rows, 4 * width), (rows, width)
    return call(
        spatial_forward_kernel, (tokens, cotangent, w, wo),
        (slab, (HEADS + 3, rows, rows)), [HBM] * 4, [VM, HBM],
        [square, square, w.shape, wo.shape, wide, (HEADS, rows, rows)],
        7 + HEADS, 2_000_000_000, 1_600_000, None,
    )


def temporal_kernel(
    factor, slab_ref, w_ref, wo_ref, branch_ref, normed_ref, go_ref, dct_ref, sems,
):
    frames, _, patches, width = slab_ref.shape
    rows = frames * patches
    hw = width // HEADS
    gather = regroup(rows, frames, patches)
    x = mm(gather, slab_ref[:, 0].reshape(rows, width))
    cot = mm(gather, slab_ref[:, 1].reshape(rows, width)).astype(B16)
    scaled, inverse = normalize(x)
    normed = scaled.astype(B16)
    normed_ref[...] = normed
    comb = mm(normed, w_ref[...]).astype(B16)
    g = mm(cot, wo_ref[...], NT).astype(B16)
    q = comb[:, :width] * (hw ** -0.5)
    k = comb[:, width : 2 * width]
    v = comb[:, 2 * width :]
    qt, kt, vt, gt = q.T, k.T, v.T, g.T
    dqt_parts, att_parts, dk_parts, dv_parts = [], [], [], []
    for patch in range(patches):
        here = slice(patch * frames, (patch + 1) * frames)
        dqt_p, att_p, dk_p, dv_p = [], [], [], []
        for pair in range(HEADS // 2):
            lanes = slice(pair * 2 * hw, (pair + 1) * 2 * hw)
            p = softmax_rows(mm(k[here, lanes], both_heads(qt[lanes, here], hw, 0, 1)))
            dp = mm(v[here, lanes], both_heads(gt[lanes, here], hw, 0, 1))
            ds = score_back(p, dp)
            for sub in range(2):
                own = slice((2 * pair + sub) * hw, (2 * pair + sub + 1) * hw)
                cols = slice(sub * frames, (sub + 1) * frames)
                att_p.append(mm(vt[own, here], p[:, cols]).astype(B16))
                dqt_p.append((mm(kt[own, here], ds[:, cols]) * (hw ** -0.5)).astype(B16))
            dk_p.append(mm(ds, both_heads(q[here, lanes], hw, 1, 0)).astype(B16))
            dv_p.append(mm(p, both_heads(g[here, lanes], hw, 1, 0)).astype(B16))
        dqt_parts.append(jnp.concatenate(dqt_p, 0))
        att_parts.append(jnp.concatenate(att_p, 0))
        dk_parts.append(jnp.concatenate(dk_p, 1))
        dv_parts.append(jnp.concatenate(dv_p, 1))
    dqt = jnp.concatenate(dqt_parts, 1)
    att = jnp.concatenate(att_parts, 1).T
    go_ref[...] = (mm(cot.T, att) * factor).astype(B16)
    dk = jnp.concatenate(dk_parts, 0)
    dv = jnp.concatenate(dv_parts, 0)
    dct_ref[:width] = dqt
    dct_ref[width : 2 * width] = dk.T
    dct_ref[2 * width :] = dv.T
    u = (
        mm(dqt.T, w_ref[:, :width], NT)
        + mm(dk, w_ref[:, width : 2 * width], NT)
        + mm(dv, w_ref[:, 2 * width :], NT)
    )
    branch = normalize_back(scaled, inverse, u).astype(B16)
    scatter = regroup(rows, patches, frames)
    branch_ref[...] = mm(scatter, branch).astype(B16).reshape(branch_ref.shape)


def temporal(factor, slab, w, wo):
    frames, _, patches, width = slab.shape
    rows = frames * patches
    return call(
        functools.partial(temporal_kernel, factor), (slab, w, wo),
        ((frames, patches, width), (rows, width), wo.shape, (3 * width, rows)),
        [VM] * 3, [VM] * 4, [], 1, 3_000_000_000, 400_000, 48,
    )


def exchange_order(cores, depth, rows, a, b):
    each = a + b
    pair = rows // each
    row = lax.broadcasted_iota(jnp.int32, (cores * depth * rows, 1), 0)
    slab = lax.shift_right_logical(row * ((1 << 16) // each + 1), 16)
    i = row - slab * each
    yh = slab & (pair - 1)
    z = lax.shift_right_logical(slab, pair.bit_length() - 1) & (depth - 1)
    core = lax.shift_right_logical(slab, (pair * depth).bit_length() - 1)
    member = (yh * depth + z) * cores + core
    source = jnp.where(i < a, member * a + i, cores * depth * pair * a + member * b + i - a)
    column = lax.broadcasted_iota(jnp.int32, (row.shape[0], row.shape[0]), 1)
    return (column == source).astype(F32).astype(B16)


def spread(gq, go, slab_ref, own_ref, send_ref):
    here = lax.axis_index("seq") % slab_ref.shape[0]
    groups = slab_ref.shape[1]
    a, b = gq.shape[0] // groups, go.shape[0] // groups
    cores, _, depth, rows, _ = slab_ref.shape
    each = a // (cores * depth * 2), b // (cores * depth * 2)
    onehot = exchange_order(cores, depth, rows, *each)
    for x in range(groups):
        source = jnp.concatenate([gq[x * a : (x + 1) * a], go[x * b : (x + 1) * b]], 0)
        moved = mm(onehot, source).astype(B16)
        slab_ref[:, x] = moved.reshape(slab_ref.shape[:1] + slab_ref.shape[2:])
        send_ref[x] = slab_ref[1 - here, x]
        own_ref[x] = slab_ref[here, x]


def weight_kernel(factor, normed_ref, go_ref, dct_ref, own_ref, send_ref, slab_ref, _):
    gq = (mm(dct_ref[...], normed_ref[...]) * factor).astype(B16)
    spread(gq, go_ref[...], slab_ref, own_ref, send_ref)


def weight_slabs(factor, normed, go, dct, shape):
    return call(
        functools.partial(weight_kernel, factor), (normed, go, dct),
        (shape[1:], shape[1:]), [VM] * 3, [VM] * 2, [shape], 1, 1_500_000_000, 0, 48,
    )


def spatial_backward_kernel(
    factor, ct_ref, br_ref, wo_ref, saved_hbm, tok_ref,
    own_ref, send_ref, sg_ref, dcomb_ref,
    comb_ref, probs_ref, slab_ref, sems,
):
    copies = Copies(sems)
    rows, width = ct_ref.shape
    comb_in = [
        copies.start(saved_hbm.at[HEADS + part], comb_ref.at[:, part * rows : (part + 1) * rows])
        for part in (2, 0, 1)
    ]
    probs_in = [copies.start(saved_hbm.at[h], probs_ref.at[h]) for h in range(HEADS)]
    hw = width // HEADS
    branch = br_ref[...].reshape(rows, width)
    sg = (ct_ref[...].astype(F32) + branch.astype(F32)).astype(B16)
    sg_ref[...] = sg
    g = mm(sg, wo_ref[...], NT).astype(B16)
    gt = g.T
    scaled, _ = normalize(tok_ref[...].astype(F32))
    normed = scaled.astype(B16)
    for copy in comb_in + probs_in:
        copy.wait()
    q = comb_ref[:, :width] * (hw ** -0.5)
    kt = comb_ref[:, width : 2 * width].T
    dqt_parts, dk_parts, dv_parts = [], [], []
    for pair in range(HEADS // 2):
        lanes = slice(pair * 2 * hw, (pair + 1) * 2 * hw)
        values = comb_ref[:, 2 * width + pair * 2 * hw : 2 * width + (pair + 1) * 2 * hw]
        dk = dv = 0.0
        for sub in range(2):
            head = 2 * pair + sub
            p = probs_ref[head]
            ds = score_back(p, mm(values, one_head(gt[lanes], sub, hw, 0)))
            dqt = mm(kt[head * hw : (head + 1) * hw], ds) * (hw ** -0.5)
            dqt_parts.append(dqt.astype(B16))
            dk = dk + mm(ds, one_head(q[:, lanes], sub, hw, 1))
            dv = dv + mm(p, one_head(g[:, lanes], sub, hw, 1))
        dk_parts.append(dk.astype(B16))
        dv_parts.append(dv.astype(B16))
    dqt = jnp.concatenate(dqt_parts, 0)
    dk = jnp.concatenate(dk_parts, 1)
    dv = jnp.concatenate(dv_parts, 1)
    dct = jnp.concatenate([dqt, dk.T, dv.T], 0)
    gq = (mm(dct, normed) * factor).astype(B16)
    go = (mm(sg.T, comb_ref[:, 3 * width :]) * factor).astype(B16)
    spread(gq, go, slab_ref, own_ref, send_ref)
    dcomb_ref[:, :width] = dqt.T
    dcomb_ref[:, width : 2 * width] = dk
    dcomb_ref[:, 2 * width :] = dv


def spatial_backward(factor, ct, branch, wo, saved, tokens, shape):
    rows, width = tokens.shape
    arrays = (ct, branch, wo, saved, tokens)
    square, wide = (rows, width), (rows, 3 * width)
    return call(
        functools.partial(spatial_backward_kernel, factor), arrays,
        (shape[1:], shape[1:], square, wide),
        [VM, VM, VM, HBM, VM], [VM] * 4,
        [(rows, 4 * width), (HEADS, rows, rows), shape], 3 + HEADS, 4_000_000_000, 0, 48,
    )


def token_kernel(tok_ref, w_ref, dcomb_ref, sg_ref, out_ref, _):
    scaled, inverse = normalize(tok_ref[...].astype(F32))
    u = mm(dcomb_ref[...], w_ref[...], NT)
    out_ref[...] = (sg_ref[...].astype(F32) + normalize_back(scaled, inverse, u)).astype(B16)


def token_gradient(tokens, w, dcomb, sg):
    return call(
        token_kernel, (tokens, w, dcomb, sg), (tokens.shape,),
        [VM] * 4, [VM], [], 1, 500_000_000, 0, 48,
    )[0]


SEQ = (("x", 4), ("yh", 2), ("z", 8), ("core", 2))


def seq_size():
    return lax.axis_size("seq")


def place(name):
    stride = 1
    for member, size in reversed(SEQ):
        if member == name:
            return stride, size
        stride *= size


def coordinate(name):
    stride, size = place(name)
    return lax.axis_index("seq") // stride % size


def shift(array, name, step):
    stride, size = place(name)
    pairs = []
    for index in range(seq_size()):
        at = index // stride % size
        pairs.append((index, index + ((at + step) % size - at) * stride))
    return lax.ppermute(array, "seq", pairs)


def slab_shape(width):
    sizes = dict(SEQ)
    rows = sizes["yh"] * 4 * width // seq_size()
    return (sizes["core"], sizes["x"], sizes["z"], rows, width)


def total_of(refs):
    here = coordinate("x")
    total = refs[0][here].astype(F32)
    for ref in refs[1:]:
        total = total + ref[...].astype(F32)
    return total.astype(B16)


def sum_kernel(*refs):
    refs[-2][...] = total_of(refs[:-2])


def join_kernel(early_ref, *refs):
    out_ref = refs[-2]
    late, early = total_of(refs[:-2]), early_ref[...]
    pair, rows = out_ref.shape[0], out_ref.shape[2] // 2
    for yh in range(pair):
        part = slice(yh * rows, (yh + 1) * rows)
        out_ref[yh] = jnp.concatenate([late[:, part], early[:, part]], 1)


def first_stages(own, send):
    part = (own.astype(F32) + shift(send, "core", 1).astype(F32)).astype(B16)
    here, size = coordinate("x"), part.shape[0]
    return (part,) + tuple(
        shift(lax.dynamic_index_in_dim(part, (here + k) % size, 0, keepdims=False), "x", k)
        for k in range(1, size)
    )


def sum_early(parts):
    return call(
        sum_kernel, parts, (parts[0].shape[1:],), [VM] * len(parts), [VM], [],
        1, 1_000_000, 0, 48,
    )[0]


def join(early, parts):
    z, rows, width = early.shape
    return call(
        join_kernel, (early, *parts), ((2, z, rows, width),), [VM] * (1 + len(parts)),
        [VM], [], 1, 1_000_000, 0, 48,
    )[0]


def groups_of(*names):
    wanted = [place(name) for name in names]
    groups = []
    for index in range(seq_size()):
        if all(index // stride % size == 0 for stride, size in wanted):
            members = [index]
            for stride, size in wanted:
                members = [at + k * stride for at in members for k in range(size)]
            groups.append(members)
    return groups


def last_stages(part):
    yh, z = part.shape[:2]
    flat = part.reshape(yh * z, *part.shape[2:])
    got = lax.all_to_all(
        flat, "seq", split_axis=0, concat_axis=0, tiled=True, axis_index_groups=groups_of("yh", "z")
    )
    mine = jnp.sum(got.astype(F32), 0).astype(B16)
    other = lax.ppermute(mine, "dp", [(0, 1), (1, 0)])
    return mine.astype(F32) + other.astype(F32)


def on_device(tokens, cotangent, wqkv_spatial, wo_spatial, wqkv_temporal, wo_temporal):
    clips, frames, patches, width = tokens.shape
    factor = (clips * frames * patches * lax.axis_size("dp") * seq_size()) ** (-0.5)
    shape = slab_shape(width)
    tok = tokens.reshape(patches, width)
    cot = cotangent.reshape(patches, width)
    traded = (seq_size(), 2, patches // seq_size(), width)

    def trade(array):
        return lax.all_to_all(array, "seq", split_axis=0, concat_axis=0, tiled=True)

    stream, saved = spatial_forward(tok, cot, wqkv_spatial, wo_spatial, traded)
    branch, normed_t, go_t, dct = temporal(factor, trade(stream), wqkv_temporal, wo_temporal)
    branch = trade(branch)
    own, send = weight_slabs(factor, normed_t, go_t, dct, shape)
    half_t = first_stages(own, send)
    own, send, stream_grad, dcomb = spatial_backward(
        factor, cot, branch, wo_spatial, saved, tok, shape
    )
    half_s = first_stages(own, send)
    token_grad = token_gradient(tok, wqkv_spatial, dcomb, stream_grad)
    half_t = sum_early(half_t)
    joined = join(half_t, half_s)
    own = last_stages(joined)
    a, b = 3 * width // seq_size(), width // seq_size()
    shares = (own[:a].T, own[a : a + b].T, own[a + b : 2 * a + b].T, own[2 * a + b :].T)
    return (token_grad.reshape(tokens.shape), *shares)


def solution(mesh):
    in_specs = (P("dp", "seq", None, None), P("dp", "seq", None, None), P(), P(), P(), P())
    out_specs = (
        P("dp", "seq", None, None),
        P(None, "seq"),
        P(None, "seq"),
        P(None, "seq"),
        P(None, "seq"),
    )
    return jax.shard_map(
        on_device, mesh=mesh, in_specs=in_specs, out_specs=out_specs, check_vma=False
    )
```

```python
import functools

import jax
import jax.numpy as jnp
from jax import lax
from jax.experimental import pallas as pl
from jax.experimental.pallas import tpu as pltpu
from jax.sharding import PartitionSpec as P

HEADS = 6
F32 = jnp.float32
B16 = jnp.bfloat16
NN = (((1,), (0,)), ((), ()))
NT = (((1,), (1,)), ((), ()))
VM = pl.BlockSpec(memory_space=pltpu.VMEM)


def mm(left, right, dims=NN):
    return lax.dot_general(left, right, dims, preferred_element_type=F32)


def normalize(values):
    average = jnp.mean(values, -1, keepdims=True)
    centered = values - average
    spread = jnp.mean(centered * centered, -1, keepdims=True)
    inverse = lax.rsqrt(spread + 1e-06)
    return centered * inverse, inverse


def normalize_back(scaled, inverse, upstream):
    return inverse * (
        upstream
        - jnp.mean(upstream, -1, keepdims=True)
        - scaled * jnp.mean(upstream * scaled, -1, keepdims=True)
    )


def one_head(block, sub, half, rows_axis):
    at = lax.broadcasted_iota(jnp.int32, block.shape, rows_axis)
    keep = (at < half) if sub == 0 else (at >= half)
    return jnp.where(keep, block, jnp.zeros_like(block))


def softmax_rows(scores):
    e = jnp.exp(scores - jnp.max(scores, 0, keepdims=True))
    return (e * (1.0 / jnp.sum(e, 0, keepdims=True))).astype(B16)


def score_back(probs, prob_grad):
    weights = probs.astype(F32)
    total = jnp.sum(weights * prob_grad, 0, keepdims=True)
    return (weights * (prob_grad - total)).astype(B16)


def both_heads(block, half, rows_axis, join_axis):
    return jnp.concatenate(
        [one_head(block, 0, half, rows_axis), one_head(block, 1, half, rows_axis)], join_axis
    )


def regroup(count, inner, outer):
    row = lax.broadcasted_iota(jnp.int32, (count, count), 0)
    column = lax.broadcasted_iota(jnp.int32, (count, count), 1)
    source = (row & (inner - 1)) * outer + lax.shift_right_logical(row, inner.bit_length() - 1)
    return (column == source).astype(F32).astype(B16)


def by_patch(onehot, block, patches):
    size = onehot.shape[0]
    some = size // patches
    moved = [mm(onehot, block[at : at + size]) for at in range(0, block.shape[0], size)]
    return jnp.concatenate(
        [part[p * some : (p + 1) * some] for p in range(patches) for part in moved], 0
    )


def by_frame(onehot, block, patches):
    size = onehot.shape[0]
    some, frames = size // patches, block.shape[0] // patches
    parts = []
    for at in range(0, frames, some):
        rows = [block[p * frames + at : p * frames + at + some] for p in range(patches)]
        parts.append(mm(onehot, jnp.concatenate(rows, 0)))
    return jnp.concatenate(parts, 0)


HBM = pl.BlockSpec(memory_space=pltpu.HBM)


def call(kernel, arrays, outs, in_specs, out_specs, scratch, copies, flops, exps=0, limit=None):
    return pl.pallas_call(
        kernel,
        out_shape=tuple(jax.ShapeDtypeStruct(shape, B16) for shape in outs),
        in_specs=in_specs,
        out_specs=tuple(out_specs),
        scratch_shapes=[pltpu.VMEM(shape, B16) for shape in scratch]
        + [pltpu.SemaphoreType.DMA((copies,))],
        compiler_params=pltpu.CompilerParams(vmem_limit_bytes=limit and limit << 20),
        cost_estimate=pl.CostEstimate(
            flops=flops,
            bytes_accessed=sum(array.size * 2 for array in arrays),
            transcendentals=exps,
        ),
    )(*arrays)


class Copies:
    def __init__(self, sems):
        self.sems, self.pending = sems, []

    def start(self, source, target):
        copy = pltpu.make_async_copy(source, target, self.sems.at[len(self.pending)])
        self.pending.append(copy)
        copy.start()
        return copy


def spatial_forward_kernel(
    tok_hbm, cot_hbm, w_hbm, wo_hbm, slab_ref, saved_hbm,
    tok_ref, cot_ref, w_ref, wo_ref, wide_ref, probs_ref, sems,
):
    copies = Copies(sems)
    tok_in = copies.start(tok_hbm, tok_ref)
    w_in = copies.start(w_hbm, w_ref)
    wo_in = copies.start(wo_hbm, wo_ref)
    cot_in = copies.start(cot_hbm, cot_ref)
    width = tok_ref.shape[-1]
    hw = width // HEADS
    outs = []
    tok_in.wait()
    x = tok_ref[...].astype(F32)
    scaled, _ = normalize(x)
    w_in.wait()
    comb = mm(scaled.astype(B16), w_ref[...]).astype(B16)
    wide_ref[:, : 3 * width] = comb
    rows = comb.shape[0]
    for part in range(2):
        outs.append(
            copies.start(wide_ref.at[:, part * rows : (part + 1) * rows], saved_hbm.at[HEADS + part])
        )
    qt = (comb[:, :width] * (hw ** -0.5)).T
    vt = comb[:, 2 * width :].T

    def scores_of(head):
        at = head // 2 * 2 * hw
        keys = comb[:, width + at : width + at + 2 * hw]
        return mm(keys, one_head(qt[at : at + 2 * hw], head % 2, hw, 0))

    parts, probs = [], []
    ahead = scores_of(0)
    for head in range(HEADS + 1):
        if head < HEADS:
            scores = ahead
            if head + 1 < HEADS:
                ahead = scores_of(head + 1)
            probs.append(softmax_rows(scores))
            probs_ref[head] = probs[head]
            outs.append(copies.start(probs_ref.at[head], saved_hbm.at[head]))
        if head:
            own = slice((head - 1) * hw, head * hw)
            parts.append(mm(vt[own], probs[head - 1]).astype(B16))
    att = jnp.concatenate(parts, 0).T
    wide_ref[:, 3 * width :] = att
    outs.append(copies.start(wide_ref.at[:, 2 * rows :], saved_hbm.at[HEADS + 2]))
    wo_in.wait()
    out = (x + mm(att, wo_ref[...])).astype(B16)
    cot_in.wait()
    half = (slab_ref.shape[0],) + slab_ref.shape[2:]
    slab_ref[:, 0] = out.reshape(half)
    slab_ref[:, 1] = cot_ref[...].reshape(half)
    for copy in outs:
        copy.wait()


def spatial_forward(tokens, cotangent, w, wo, slab):
    rows, width = tokens.shape
    wide, square = (rows, 4 * width), (rows, width)
    return call(
        spatial_forward_kernel, (tokens, cotangent, w, wo),
        (slab, (HEADS + 3, rows, rows)), [HBM] * 4, [VM, HBM],
        [square, square, w.shape, wo.shape, wide, (HEADS, rows, rows)],
        7 + HEADS, 2_000_000_000, 1_600_000, None,
    )


def temporal_kernel(
    factor, slab_ref, w_ref, wo_ref, branch_ref, normed_ref, go_ref, dct_ref, sems,
):
    frames, _, patches, width = slab_ref.shape
    rows = frames * patches
    hw = width // HEADS
    size = min(rows, 256)
    gather = regroup(size, size // patches, patches)
    x = by_patch(gather, slab_ref[:, 0].reshape(rows, width), patches)
    cot = by_patch(gather, slab_ref[:, 1].reshape(rows, width), patches).astype(B16)
    scaled, inverse = normalize(x)
    normed = scaled.astype(B16)
    normed_ref[...] = normed
    comb = mm(normed, w_ref[...]).astype(B16)
    g = mm(cot, wo_ref[...], NT).astype(B16)
    q = comb[:, :width] * (hw ** -0.5)
    k = comb[:, width : 2 * width]
    v = comb[:, 2 * width :]
    qt, kt, vt, gt = q.T, k.T, v.T, g.T
    groups = [
        (slice(patch * frames, (patch + 1) * frames), slice(pair * 2 * hw, (pair + 1) * 2 * hw))
        for patch in range(patches)
        for pair in range(HEADS // 2)
    ]
    scores = [mm(k[here, lanes], both_heads(qt[lanes, here], hw, 0, 1)) for here, lanes in groups]
    back = [mm(v[here, lanes], both_heads(gt[lanes, here], hw, 0, 1)) for here, lanes in groups]
    probs = [softmax_rows(member) for member in scores]
    grads = [score_back(p, dp) for p, dp in zip(probs, back)]
    dk = [mm(ds, both_heads(q[at], hw, 1, 0)).astype(B16) for ds, at in zip(grads, groups)]
    dv = [mm(p, both_heads(g[at], hw, 1, 0)).astype(B16) for p, at in zip(probs, groups)]
    att, dqt = [], []
    for p, ds, (here, lanes) in zip(probs, grads, groups):
        for sub in range(2):
            own = slice(lanes.start + sub * hw, lanes.start + (sub + 1) * hw)
            cols = slice(sub * frames, (sub + 1) * frames)
            att.append(mm(vt[own, here], p[:, cols]).astype(B16))
            dqt.append((mm(kt[own, here], ds[:, cols]) * (hw ** -0.5)).astype(B16))

    def by_patch_of(parts, axis):
        each = len(parts) // patches
        return [
            jnp.concatenate(parts[n * each : (n + 1) * each], axis) for n in range(patches)
        ]

    dqt_parts, att_parts = by_patch_of(dqt, 0), by_patch_of(att, 0)
    dk_parts, dv_parts = by_patch_of(dk, 1), by_patch_of(dv, 1)
    dqt = jnp.concatenate(dqt_parts, 1)
    att = jnp.concatenate(att_parts, 1).T
    go_ref[...] = (mm(cot.T, att) * factor).astype(B16)
    dk = jnp.concatenate(dk_parts, 0)
    dv = jnp.concatenate(dv_parts, 0)
    dct_ref[:width] = dqt
    dct_ref[width : 2 * width] = dk.T
    dct_ref[2 * width :] = dv.T
    u = (
        mm(dqt.T, w_ref[:, :width], NT)
        + mm(dk, w_ref[:, width : 2 * width], NT)
        + mm(dv, w_ref[:, 2 * width :], NT)
    )
    branch = normalize_back(scaled, inverse, u).astype(B16)
    scatter = regroup(size, patches, size // patches)
    branch = by_frame(scatter, branch, patches).astype(B16)
    branch_ref[...] = branch.reshape(branch_ref.shape)


def temporal(factor, slab, w, wo):
    frames, _, patches, width = slab.shape
    rows = frames * patches
    return call(
        functools.partial(temporal_kernel, factor), (slab, w, wo),
        ((frames, patches, width), (rows, width), wo.shape, (3 * width, rows)),
        [VM] * 3, [VM] * 4, [], 1, 3_000_000_000, 400_000, 48,
    )


def exchange_order(cores, depth, rows, a, b):
    each = a + b
    pair = rows // each
    row = lax.broadcasted_iota(jnp.int32, (cores * depth * rows, 1), 0)
    slab = lax.shift_right_logical(row * ((1 << 16) // each + 1), 16)
    i = row - slab * each
    yh = slab & (pair - 1)
    z = lax.shift_right_logical(slab, pair.bit_length() - 1) & (depth - 1)
    core = lax.shift_right_logical(slab, (pair * depth).bit_length() - 1)
    member = (yh * depth + z) * cores + core
    source = jnp.where(i < a, member * a + i, cores * depth * pair * a + member * b + i - a)
    column = lax.broadcasted_iota(jnp.int32, (row.shape[0], row.shape[0]), 1)
    return (column == source).astype(F32).astype(B16)


def spread(gq, go, slab_ref, own_ref, send_ref):
    here = lax.axis_index("seq") % slab_ref.shape[0]
    groups = slab_ref.shape[1]
    a, b = gq.shape[0] // groups, go.shape[0] // groups
    cores, _, depth, rows, _ = slab_ref.shape
    each = a // (cores * depth * 2), b // (cores * depth * 2)
    onehot = exchange_order(cores, depth, rows, *each)
    for x in range(groups):
        source = jnp.concatenate([gq[x * a : (x + 1) * a], go[x * b : (x + 1) * b]], 0)
        moved = mm(onehot, source).astype(B16)
        slab_ref[:, x] = moved.reshape(slab_ref.shape[:1] + slab_ref.shape[2:])
        send_ref[x] = slab_ref[1 - here, x]
        own_ref[x] = slab_ref[here, x]


def weight_kernel(factor, normed_ref, go_ref, dct_ref, own_ref, send_ref, slab_ref, _):
    gq = (mm(dct_ref[...], normed_ref[...]) * factor).astype(B16)
    spread(gq, go_ref[...], slab_ref, own_ref, send_ref)


def weight_slabs(factor, normed, go, dct, shape):
    return call(
        functools.partial(weight_kernel, factor), (normed, go, dct),
        (shape[1:], shape[1:]), [VM] * 3, [VM] * 2, [shape], 1, 1_500_000_000, 0, 48,
    )


def spatial_backward_kernel(
    factor, ct_ref, br_ref, wo_ref, saved_hbm, tok_ref,
    own_ref, send_ref, sg_ref, dcomb_ref,
    comb_ref, probs_ref, slab_ref, sems,
):
    copies = Copies(sems)
    rows, width = ct_ref.shape
    comb_in = [
        copies.start(saved_hbm.at[HEADS + part], comb_ref.at[:, part * rows : (part + 1) * rows])
        for part in (2, 0, 1)
    ]
    probs_in = [copies.start(saved_hbm.at[h], probs_ref.at[h]) for h in range(HEADS)]
    hw = width // HEADS
    branch = br_ref[...].reshape(rows, width)
    sg = (ct_ref[...].astype(F32) + branch.astype(F32)).astype(B16)
    sg_ref[...] = sg
    g = mm(sg, wo_ref[...], NT).astype(B16)
    gt = g.T
    scaled, _ = normalize(tok_ref[...].astype(F32))
    normed = scaled.astype(B16)
    for copy in comb_in + probs_in:
        copy.wait()
    q = comb_ref[:, :width] * (hw ** -0.5)
    kt = comb_ref[:, width : 2 * width].T

    def back_of(head):
        at = head // 2 * 2 * hw
        values = comb_ref[:, 2 * width + at : 2 * width + at + 2 * hw]
        return mm(values, one_head(gt[at : at + 2 * hw], head % 2, hw, 0))

    dqt_parts, dk_parts, dv_parts, grads = [], [], [], []
    ahead = back_of(0)
    for step in range(HEADS + 1):
        if step < HEADS:
            dp = ahead
            if step + 1 < HEADS:
                ahead = back_of(step + 1)
            grads.append(score_back(probs_ref[step], dp))
        if not step:
            continue
        head, sub = step - 1, (step - 1) % 2
        lanes = slice(head // 2 * 2 * hw, (head // 2 + 1) * 2 * hw)
        ds = grads[head]
        dqt = mm(kt[head * hw : (head + 1) * hw], ds) * (hw ** -0.5)
        dqt_parts.append(dqt.astype(B16))
        dk = mm(ds, one_head(q[:, lanes], sub, hw, 1))
        dv = mm(probs_ref[head], one_head(g[:, lanes], sub, hw, 1))
        if sub:
            dk_parts.append((dk_first + dk).astype(B16))
            dv_parts.append((dv_first + dv).astype(B16))
        dk_first, dv_first = dk, dv
    dqt = jnp.concatenate(dqt_parts, 0)
    dk = jnp.concatenate(dk_parts, 1)
    dv = jnp.concatenate(dv_parts, 1)
    dct = jnp.concatenate([dqt, dk.T, dv.T], 0)
    gq = (mm(dct, normed) * factor).astype(B16)
    go = (mm(sg.T, comb_ref[:, 3 * width :]) * factor).astype(B16)
    spread(gq, go, slab_ref, own_ref, send_ref)
    dcomb_ref[:, :width] = dqt.T
    dcomb_ref[:, width : 2 * width] = dk
    dcomb_ref[:, 2 * width :] = dv


def spatial_backward(factor, ct, branch, wo, saved, tokens, shape):
    rows, width = tokens.shape
    arrays = (ct, branch, wo, saved, tokens)
    square, wide = (rows, width), (rows, 3 * width)
    return call(
        functools.partial(spatial_backward_kernel, factor), arrays,
        (shape[1:], shape[1:], square, wide),
        [VM, VM, VM, HBM, VM], [VM] * 4,
        [(rows, 4 * width), (HEADS, rows, rows), shape], 3 + HEADS, 4_000_000_000, 0, 48,
    )


def token_kernel(tok_ref, w_ref, dcomb_ref, sg_ref, out_ref, _):
    scaled, inverse = normalize(tok_ref[...].astype(F32))
    u = mm(dcomb_ref[...], w_ref[...], NT)
    out_ref[...] = (sg_ref[...].astype(F32) + normalize_back(scaled, inverse, u)).astype(B16)


def token_gradient(tokens, w, dcomb, sg):
    return call(
        token_kernel, (tokens, w, dcomb, sg), (tokens.shape,),
        [VM] * 4, [VM], [], 1, 500_000_000, 0, 48,
    )[0]


SEQ = (("x", 4), ("yh", 2), ("z", 8), ("core", 2))


def seq_size():
    return lax.axis_size("seq")


def place(name):
    stride = 1
    for member, size in reversed(SEQ):
        if member == name:
            return stride, size
        stride *= size


def coordinate(name):
    stride, size = place(name)
    return lax.axis_index("seq") // stride % size


def shift(array, name, step):
    stride, size = place(name)
    pairs = []
    for index in range(seq_size()):
        at = index // stride % size
        pairs.append((index, index + ((at + step) % size - at) * stride))
    return lax.ppermute(array, "seq", pairs)


def slab_shape(width):
    sizes = dict(SEQ)
    rows = sizes["yh"] * 4 * width // seq_size()
    return (sizes["core"], sizes["x"], sizes["z"], rows, width)


def total_of(refs):
    here = coordinate("x")
    total = refs[0][here].astype(F32)
    for ref in refs[1:]:
        total = total + ref[...].astype(F32)
    return total.astype(B16)


def sum_kernel(*refs):
    refs[-2][...] = total_of(refs[:-2])


def join_kernel(early_ref, *refs):
    out_ref = refs[-2]
    late, early = total_of(refs[:-2]), early_ref[...]
    pair, rows = out_ref.shape[0], out_ref.shape[2] // 2
    for yh in range(pair):
        part = slice(yh * rows, (yh + 1) * rows)
        out_ref[yh] = jnp.concatenate([late[:, part], early[:, part]], 1)


def first_stages(own, send):
    part = (own.astype(F32) + shift(send, "core", 1).astype(F32)).astype(B16)
    here, size = coordinate("x"), part.shape[0]
    return (part,) + tuple(
        shift(lax.dynamic_index_in_dim(part, (here + k) % size, 0, keepdims=False), "x", k)
        for k in range(1, size)
    )


def sum_early(parts):
    return call(
        sum_kernel, parts, (parts[0].shape[1:],), [VM] * len(parts), [VM], [],
        1, 1_000_000, 0, 48,
    )[0]


def join(early, parts):
    z, rows, width = early.shape
    return call(
        join_kernel, (early, *parts), ((2, z, rows, width),), [VM] * (1 + len(parts)),
        [VM], [], 1, 1_000_000, 0, 48,
    )[0]


def groups_of(*names):
    wanted = [place(name) for name in names]
    groups = []
    for index in range(seq_size()):
        if all(index // stride % size == 0 for stride, size in wanted):
            members = [index]
            for stride, size in wanted:
                members = [at + k * stride for at in members for k in range(size)]
            groups.append(members)
    return groups


def last_stages(part):
    yh, z = part.shape[:2]
    flat = part.reshape(yh * z, *part.shape[2:])
    got = lax.all_to_all(
        flat, "seq", split_axis=0, concat_axis=0, tiled=True, axis_index_groups=groups_of("yh", "z")
    )
    mine = jnp.sum(got.astype(F32), 0).astype(B16)
    other = lax.ppermute(mine, "dp", [(0, 1), (1, 0)])
    return mine.astype(F32) + other.astype(F32)


def on_device(tokens, cotangent, wqkv_spatial, wo_spatial, wqkv_temporal, wo_temporal):
    clips, frames, patches, width = tokens.shape
    factor = (clips * frames * patches * lax.axis_size("dp") * seq_size()) ** (-0.5)
    shape = slab_shape(width)
    tok = tokens.reshape(patches, width)
    cot = cotangent.reshape(patches, width)
    traded = (seq_size(), 2, patches // seq_size(), width)

    def trade(array):
        return lax.all_to_all(array, "seq", split_axis=0, concat_axis=0, tiled=True)

    stream, saved = spatial_forward(tok, cot, wqkv_spatial, wo_spatial, traded)
    branch, normed_t, go_t, dct = temporal(factor, trade(stream), wqkv_temporal, wo_temporal)
    branch = trade(branch)
    own, send = weight_slabs(factor, normed_t, go_t, dct, shape)
    half_t = first_stages(own, send)
    own, send, stream_grad, dcomb = spatial_backward(
        factor, cot, branch, wo_spatial, saved, tok, shape
    )
    half_s = first_stages(own, send)
    token_grad = token_gradient(tok, wqkv_spatial, dcomb, stream_grad)
    half_t = sum_early(half_t)
    joined = join(half_t, half_s)
    own = last_stages(joined)
    a, b = 3 * width // seq_size(), width // seq_size()
    shares = (own[:a].T, own[a : a + b].T, own[a + b : 2 * a + b].T, own[2 * a + b :].T)
    return (token_grad.reshape(tokens.shape), *shares)


def solution(mesh):
    in_specs = (P("dp", "seq", None, None), P("dp", "seq", None, None), P(), P(), P(), P())
    out_specs = (
        P("dp", "seq", None, None),
        P(None, "seq"),
        P(None, "seq"),
        P(None, "seq"),
        P(None, "seq"),
    )
    return jax.shard_map(
        on_device, mesh=mesh, in_specs=in_specs, out_specs=out_specs, check_vma=False
    )
```

```python
import functools

import jax
import jax.numpy as jnp
from jax import lax
from jax.experimental import pallas as pl
from jax.experimental.pallas import tpu as pltpu
from jax.sharding import PartitionSpec as P

HEADS = 6
F32 = jnp.float32
B16 = jnp.bfloat16
NN = (((1,), (0,)), ((), ()))
NT = (((1,), (1,)), ((), ()))
VM = pl.BlockSpec(memory_space=pltpu.VMEM)


def mm(left, right, dims=NN):
    return lax.dot_general(left, right, dims, preferred_element_type=F32)


def normalize(values):
    average = jnp.mean(values, -1, keepdims=True)
    centered = values - average
    spread = jnp.mean(centered * centered, -1, keepdims=True)
    inverse = lax.rsqrt(spread + 1e-06)
    return centered * inverse, inverse


def normalize_back(scaled, inverse, upstream):
    return inverse * (
        upstream
        - jnp.mean(upstream, -1, keepdims=True)
        - scaled * jnp.mean(upstream * scaled, -1, keepdims=True)
    )


def one_head(block, sub, half, rows_axis):
    at = lax.broadcasted_iota(jnp.int32, block.shape, rows_axis)
    keep = (at < half) if sub == 0 else (at >= half)
    return jnp.where(keep, block, jnp.zeros_like(block))


def softmax_rows(scores):
    e = jnp.exp(scores - jnp.max(scores, 0, keepdims=True))
    return (e * (1.0 / jnp.sum(e, 0, keepdims=True))).astype(B16)


def score_back(probs, prob_grad):
    weights = probs.astype(F32)
    total = jnp.sum(weights * prob_grad, 0, keepdims=True)
    return (weights * (prob_grad - total)).astype(B16)


def both_heads(block, half, rows_axis, join_axis):
    return jnp.concatenate(
        [one_head(block, 0, half, rows_axis), one_head(block, 1, half, rows_axis)], join_axis
    )


def regroup(count, inner, outer):
    row = lax.broadcasted_iota(jnp.int32, (count, count), 0)
    column = lax.broadcasted_iota(jnp.int32, (count, count), 1)
    source = (row & (inner - 1)) * outer + lax.shift_right_logical(row, inner.bit_length() - 1)
    return (column == source).astype(F32).astype(B16)


def by_patch(onehot, block, patches):
    size = onehot.shape[0]
    some = size // patches
    moved = [mm(onehot, block[at : at + size]) for at in range(0, block.shape[0], size)]
    return jnp.concatenate(
        [part[p * some : (p + 1) * some] for p in range(patches) for part in moved], 0
    )


def by_frame(onehot, block, patches):
    size = onehot.shape[0]
    some, frames = size // patches, block.shape[0] // patches
    parts = []
    for at in range(0, frames, some):
        rows = [block[p * frames + at : p * frames + at + some] for p in range(patches)]
        parts.append(mm(onehot, jnp.concatenate(rows, 0)))
    return jnp.concatenate(parts, 0)


HBM = pl.BlockSpec(memory_space=pltpu.HBM)


def call(kernel, arrays, outs, in_specs, out_specs, scratch, copies, flops, exps=0, limit=None):
    return pl.pallas_call(
        kernel,
        out_shape=tuple(jax.ShapeDtypeStruct(shape, B16) for shape in outs),
        in_specs=in_specs,
        out_specs=tuple(out_specs),
        scratch_shapes=[pltpu.VMEM(shape, B16) for shape in scratch]
        + [pltpu.SemaphoreType.DMA((copies,))],
        compiler_params=pltpu.CompilerParams(vmem_limit_bytes=limit and limit << 20),
        cost_estimate=pl.CostEstimate(
            flops=flops,
            bytes_accessed=sum(array.size * 2 for array in arrays),
            transcendentals=exps,
        ),
    )(*arrays)


class Copies:
    def __init__(self, sems):
        self.sems, self.pending = sems, []

    def start(self, source, target):
        copy = pltpu.make_async_copy(source, target, self.sems.at[len(self.pending)])
        self.pending.append(copy)
        copy.start()
        return copy


def spatial_forward_kernel(
    tok_hbm, cot_hbm, w_hbm, wo_hbm, slab_ref, saved_hbm,
    tok_ref, cot_ref, w_ref, wo_ref, wide_ref, probs_ref, sems,
):
    copies = Copies(sems)
    tok_in = copies.start(tok_hbm, tok_ref)
    w_in = copies.start(w_hbm, w_ref)
    wo_in = copies.start(wo_hbm, wo_ref)
    cot_in = copies.start(cot_hbm, cot_ref)
    width = tok_ref.shape[-1]
    hw = width // HEADS
    outs = []
    tok_in.wait()
    x = tok_ref[...].astype(F32)
    scaled, _ = normalize(x)
    w_in.wait()
    comb = mm(scaled.astype(B16), w_ref[...]).astype(B16)
    wide_ref[:, : 3 * width] = comb
    rows = comb.shape[0]
    for part in range(2):
        outs.append(
            copies.start(wide_ref.at[:, part * rows : (part + 1) * rows], saved_hbm.at[HEADS + part])
        )
    qt = (comb[:, :width] * (hw ** -0.5)).T
    vt = comb[:, 2 * width :].T

    def scores_of(head):
        at = head // 2 * 2 * hw
        keys = comb[:, width + at : width + at + 2 * hw]
        return mm(keys, one_head(qt[at : at + 2 * hw], head % 2, hw, 0))

    parts, probs = [], []
    ahead = scores_of(0)
    for head in range(HEADS + 1):
        if head < HEADS:
            scores = ahead
            if head + 1 < HEADS:
                ahead = scores_of(head + 1)
            probs.append(softmax_rows(scores))
            probs_ref[head] = probs[head]
            outs.append(copies.start(probs_ref.at[head], saved_hbm.at[head]))
        if head:
            own = slice((head - 1) * hw, head * hw)
            parts.append(mm(vt[own], probs[head - 1]).astype(B16))
    att = jnp.concatenate(parts, 0).T
    wide_ref[:, 3 * width :] = att
    outs.append(copies.start(wide_ref.at[:, 2 * rows :], saved_hbm.at[HEADS + 2]))
    wo_in.wait()
    out = (x + mm(att, wo_ref[...])).astype(B16)
    cot_in.wait()
    half = (slab_ref.shape[0],) + slab_ref.shape[2:]
    slab_ref[:, 0] = out.reshape(half)
    slab_ref[:, 1] = cot_ref[...].reshape(half)
    for copy in outs:
        copy.wait()


def spatial_forward(tokens, cotangent, w, wo, slab):
    rows, width = tokens.shape
    wide, square = (rows, 4 * width), (rows, width)
    return call(
        spatial_forward_kernel, (tokens, cotangent, w, wo),
        (slab, (HEADS + 3, rows, rows)), [HBM] * 4, [VM, HBM],
        [square, square, w.shape, wo.shape, wide, (HEADS, rows, rows)],
        7 + HEADS, 2_000_000_000, 1_600_000, None,
    )


def temporal_kernel(
    factor, slab_ref, w_ref, wo_ref, branch_ref, normed_ref, go_ref, dct_ref, sems,
):
    frames, _, patches, width = slab_ref.shape
    rows = frames * patches
    hw = width // HEADS
    size = min(rows, 256)
    gather = regroup(size, size // patches, patches)
    x = by_patch(gather, slab_ref[:, 0].reshape(rows, width), patches)
    cot = by_patch(gather, slab_ref[:, 1].reshape(rows, width), patches).astype(B16)
    scaled, inverse = normalize(x)
    normed = scaled.astype(B16)
    normed_ref[...] = normed
    comb = mm(normed, w_ref[...]).astype(B16)
    g = mm(cot, wo_ref[...], NT).astype(B16)
    q = comb[:, :width] * (hw ** -0.5)
    k = comb[:, width : 2 * width]
    v = comb[:, 2 * width :]
    qt, kt, vt, gt = q.T, k.T, v.T, g.T
    groups = [
        (slice(patch * frames, (patch + 1) * frames), slice(pair * 2 * hw, (pair + 1) * 2 * hw))
        for patch in range(patches)
        for pair in range(HEADS // 2)
    ]
    scores = [mm(k[here, lanes], both_heads(qt[lanes, here], hw, 0, 1)) for here, lanes in groups]
    back = [mm(v[here, lanes], both_heads(gt[lanes, here], hw, 0, 1)) for here, lanes in groups]
    probs = [softmax_rows(member) for member in scores]
    grads = [score_back(p, dp) for p, dp in zip(probs, back)]
    dk = [mm(ds, both_heads(q[at], hw, 1, 0)).astype(B16) for ds, at in zip(grads, groups)]
    dv = [mm(p, both_heads(g[at], hw, 1, 0)).astype(B16) for p, at in zip(probs, groups)]
    att, dqt = [], []
    for p, ds, (here, lanes) in zip(probs, grads, groups):
        for sub in range(2):
            own = slice(lanes.start + sub * hw, lanes.start + (sub + 1) * hw)
            cols = slice(sub * frames, (sub + 1) * frames)
            att.append(mm(vt[own, here], p[:, cols]).astype(B16))
            dqt.append((mm(kt[own, here], ds[:, cols]) * (hw ** -0.5)).astype(B16))

    def by_patch_of(parts, axis):
        each = len(parts) // patches
        return [
            jnp.concatenate(parts[n * each : (n + 1) * each], axis) for n in range(patches)
        ]

    dqt_parts, att_parts = by_patch_of(dqt, 0), by_patch_of(att, 0)
    dk_parts, dv_parts = by_patch_of(dk, 1), by_patch_of(dv, 1)
    dqt = jnp.concatenate(dqt_parts, 1)
    att = jnp.concatenate(att_parts, 1).T
    go_ref[...] = (mm(cot.T, att) * factor).astype(B16)
    dk = jnp.concatenate(dk_parts, 0)
    dv = jnp.concatenate(dv_parts, 0)
    dct_ref[:width] = dqt
    dct_ref[width : 2 * width] = dk.T
    dct_ref[2 * width :] = dv.T
    u = (
        mm(dqt.T, w_ref[:, :width], NT)
        + mm(dk, w_ref[:, width : 2 * width], NT)
        + mm(dv, w_ref[:, 2 * width :], NT)
    )
    branch = normalize_back(scaled, inverse, u).astype(B16)
    scatter = regroup(size, patches, size // patches)
    branch = by_frame(scatter, branch, patches).astype(B16)
    branch_ref[...] = branch.reshape(branch_ref.shape)


def temporal(factor, slab, w, wo):
    frames, _, patches, width = slab.shape
    rows = frames * patches
    return call(
        functools.partial(temporal_kernel, factor), (slab, w, wo),
        ((frames, patches, width), (rows, width), wo.shape, (3 * width, rows)),
        [VM] * 3, [VM] * 4, [], 1, 3_000_000_000, 400_000, 48,
    )


def exchange_order(cores, depth, rows, a, b):
    each = a + b
    pair = rows // each
    row = lax.broadcasted_iota(jnp.int32, (cores * depth * rows, 1), 0)
    slab = lax.shift_right_logical(row * ((1 << 16) // each + 1), 16)
    i = row - slab * each
    yh = slab & (pair - 1)
    z = lax.shift_right_logical(slab, pair.bit_length() - 1) & (depth - 1)
    core = lax.shift_right_logical(slab, (pair * depth).bit_length() - 1)
    member = (yh * depth + z) * cores + core
    source = jnp.where(i < a, member * a + i, cores * depth * pair * a + member * b + i - a)
    column = lax.broadcasted_iota(jnp.int32, (row.shape[0], row.shape[0]), 1)
    return (column == source).astype(F32).astype(B16)


def spread(gq, go, slab_ref, own_ref, send_ref):
    here = lax.axis_index("seq") % slab_ref.shape[0]
    groups = slab_ref.shape[1]
    a, b = gq.shape[0] // groups, go.shape[0] // groups
    cores, _, depth, rows, _ = slab_ref.shape
    each = a // (cores * depth * 2), b // (cores * depth * 2)
    onehot = exchange_order(cores, depth, rows, *each)
    for x in range(groups):
        source = jnp.concatenate([gq[x * a : (x + 1) * a], go[x * b : (x + 1) * b]], 0)
        moved = mm(onehot, source).astype(B16)
        slab_ref[:, x] = moved.reshape(slab_ref.shape[:1] + slab_ref.shape[2:])
        send_ref[x] = slab_ref[1 - here, x]
        own_ref[x] = slab_ref[here, x]


def weight_kernel(factor, normed_ref, go_ref, dct_ref, own_ref, send_ref, slab_ref, _):
    gq = (mm(dct_ref[...], normed_ref[...]) * factor).astype(B16)
    spread(gq, go_ref[...], slab_ref, own_ref, send_ref)


def weight_slabs(factor, normed, go, dct, shape):
    return call(
        functools.partial(weight_kernel, factor), (normed, go, dct),
        (shape[1:], shape[1:]), [VM] * 3, [VM] * 2, [shape], 1, 1_500_000_000, 0, 48,
    )


def spatial_backward_kernel(
    factor, ct_ref, br_ref, wo_ref, saved_hbm, tok_ref,
    own_ref, send_ref, sg_ref, dqt_ref, dkv_ref,
    comb_ref, probs_ref, slab_ref, sems,
):
    copies = Copies(sems)
    rows, width = ct_ref.shape
    comb_in = [
        copies.start(saved_hbm.at[HEADS + part], comb_ref.at[:, part * rows : (part + 1) * rows])
        for part in (2, 0, 1)
    ]
    probs_in = [copies.start(saved_hbm.at[h], probs_ref.at[h]) for h in range(HEADS)]
    hw = width // HEADS
    branch = br_ref[...].reshape(rows, width)
    sg = (ct_ref[...].astype(F32) + branch.astype(F32)).astype(B16)
    sg_ref[...] = sg
    g = mm(sg, wo_ref[...], NT).astype(B16)
    gt = g.T
    scaled, _ = normalize(tok_ref[...].astype(F32))
    normed = scaled.astype(B16)
    for copy in comb_in:
        copy.wait()
    go = (mm(sg.T, comb_ref[:, 3 * width :]) * factor).astype(B16)
    q = comb_ref[:, :width] * (hw ** -0.5)
    kt = comb_ref[:, width : 2 * width].T

    def back_of(head):
        at = head // 2 * 2 * hw
        values = comb_ref[:, 2 * width + at : 2 * width + at + 2 * hw]
        return mm(values, one_head(gt[at : at + 2 * hw], head % 2, hw, 0))

    dqt_parts, dk_parts, dv_parts, grads = [], [], [], []
    ahead = back_of(0)
    for copy in probs_in:
        copy.wait()
    for step in range(HEADS + 1):
        if step < HEADS:
            dp = ahead
            if step + 1 < HEADS:
                ahead = back_of(step + 1)
            grads.append(score_back(probs_ref[step], dp))
        if not step:
            continue
        head, sub = step - 1, (step - 1) % 2
        lanes = slice(head // 2 * 2 * hw, (head // 2 + 1) * 2 * hw)
        ds = grads[head]
        dqt = mm(kt[head * hw : (head + 1) * hw], ds) * (hw ** -0.5)
        dqt_parts.append(dqt.astype(B16))
        dk = mm(ds, one_head(q[:, lanes], sub, hw, 1))
        dv = mm(probs_ref[head], one_head(g[:, lanes], sub, hw, 1))
        if sub:
            dk_parts.append((dk_first + dk).astype(B16))
            dv_parts.append((dv_first + dv).astype(B16))
        dk_first, dv_first = dk, dv
    dqt = jnp.concatenate(dqt_parts, 0)
    dk = jnp.concatenate(dk_parts, 1)
    dv = jnp.concatenate(dv_parts, 1)
    dct = jnp.concatenate([dqt, dk.T, dv.T], 0)
    gq = (mm(dct, normed) * factor).astype(B16)
    spread(gq, go, slab_ref, own_ref, send_ref)
    dqt_ref[...] = dqt
    dkv_ref[:, :width] = dk
    dkv_ref[:, width:] = dv


def spatial_backward(factor, ct, branch, wo, saved, tokens, shape):
    rows, width = tokens.shape
    arrays = (ct, branch, wo, saved, tokens)
    square, wide = (rows, width), (rows, 2 * width)
    return call(
        functools.partial(spatial_backward_kernel, factor), arrays,
        (shape[1:], shape[1:], square, (width, rows), wide),
        [VM, VM, VM, HBM, VM], [VM] * 5,
        [(rows, 4 * width), (HEADS, rows, rows), shape], 3 + HEADS, 4_000_000_000, 0, 48,
    )


def token_kernel(tok_ref, w_ref, dqt_ref, dkv_ref, sg_ref, out_ref, _):
    width = tok_ref.shape[1]
    scaled, inverse = normalize(tok_ref[...].astype(F32))
    u = mm(dqt_ref[...].T, w_ref[:, :width], NT) + mm(dkv_ref[...], w_ref[:, width:], NT)
    out_ref[...] = (sg_ref[...].astype(F32) + normalize_back(scaled, inverse, u)).astype(B16)


def token_gradient(tokens, w, dqt, dkv, sg):
    return call(
        token_kernel, (tokens, w, dqt, dkv, sg), (tokens.shape,),
        [VM] * 5, [VM], [], 1, 500_000_000, 0, 48,
    )[0]


SEQ = (("x", 4), ("yh", 2), ("z", 8), ("core", 2))


def seq_size():
    return lax.axis_size("seq")


def place(name):
    stride = 1
    for member, size in reversed(SEQ):
        if member == name:
            return stride, size
        stride *= size


def coordinate(name):
    stride, size = place(name)
    return lax.axis_index("seq") // stride % size


def shift(array, name, step):
    stride, size = place(name)
    pairs = []
    for index in range(seq_size()):
        at = index // stride % size
        pairs.append((index, index + ((at + step) % size - at) * stride))
    return lax.ppermute(array, "seq", pairs)


def slab_shape(width):
    sizes = dict(SEQ)
    rows = sizes["yh"] * 4 * width // seq_size()
    return (sizes["core"], sizes["x"], sizes["z"], rows, width)


def total_of(refs):
    here = coordinate("x")
    total = refs[0][here].astype(F32)
    for ref in refs[1:]:
        total = total + ref[...].astype(F32)
    return total.astype(B16)


def sum_kernel(*refs):
    refs[-2][...] = total_of(refs[:-2])


def join_kernel(early_ref, *refs):
    out_ref = refs[-2]
    late, early = total_of(refs[:-2]), early_ref[...]
    pair, rows = out_ref.shape[0], out_ref.shape[2] // 2
    for yh in range(pair):
        part = slice(yh * rows, (yh + 1) * rows)
        out_ref[yh] = jnp.concatenate([late[:, part], early[:, part]], 1)


def first_stages(own, send):
    part = (own.astype(F32) + shift(send, "core", 1).astype(F32)).astype(B16)
    here, size = coordinate("x"), part.shape[0]
    return (part,) + tuple(
        shift(lax.dynamic_index_in_dim(part, (here + k) % size, 0, keepdims=False), "x", k)
        for k in range(1, size)
    )


def sum_early(parts):
    return call(
        sum_kernel, parts, (parts[0].shape[1:],), [VM] * len(parts), [VM], [],
        1, 1_000_000, 0, 48,
    )[0]


def join(early, parts):
    z, rows, width = early.shape
    return call(
        join_kernel, (early, *parts), ((2, z, rows, width),), [VM] * (1 + len(parts)),
        [VM], [], 1, 1_000_000, 0, 48,
    )[0]


def groups_of(*names):
    wanted = [place(name) for name in names]
    groups = []
    for index in range(seq_size()):
        if all(index // stride % size == 0 for stride, size in wanted):
            members = [index]
            for stride, size in wanted:
                members = [at + k * stride for at in members for k in range(size)]
            groups.append(members)
    return groups


def last_stages(part):
    yh, z = part.shape[:2]
    flat = part.reshape(yh * z, *part.shape[2:])
    got = lax.all_to_all(
        flat, "seq", split_axis=0, concat_axis=0, tiled=True, axis_index_groups=groups_of("yh", "z")
    )
    mine = jnp.sum(got.astype(F32), 0).astype(B16)
    other = lax.ppermute(mine, "dp", [(0, 1), (1, 0)])
    return mine.astype(F32) + other.astype(F32)


def on_device(tokens, cotangent, wqkv_spatial, wo_spatial, wqkv_temporal, wo_temporal):
    clips, frames, patches, width = tokens.shape
    factor = (clips * frames * patches * lax.axis_size("dp") * seq_size()) ** (-0.5)
    shape = slab_shape(width)
    tok = tokens.reshape(patches, width)
    cot = cotangent.reshape(patches, width)
    traded = (seq_size(), 2, patches // seq_size(), width)

    def trade(array):
        return lax.all_to_all(array, "seq", split_axis=0, concat_axis=0, tiled=True)

    stream, saved = spatial_forward(tok, cot, wqkv_spatial, wo_spatial, traded)
    branch, normed_t, go_t, dct = temporal(factor, trade(stream), wqkv_temporal, wo_temporal)
    branch = trade(branch)
    own, send = weight_slabs(factor, normed_t, go_t, dct, shape)
    half_t = first_stages(own, send)
    own, send, stream_grad, dqt, dkv = spatial_backward(
        factor, cot, branch, wo_spatial, saved, tok, shape
    )
    half_s = first_stages(own, send)
    token_grad = token_gradient(tok, wqkv_spatial, dqt, dkv, stream_grad)
    half_t = sum_early(half_t)
    joined = join(half_t, half_s)
    own = last_stages(joined)
    a, b = 3 * width // seq_size(), width // seq_size()
    shares = (own[:a].T, own[a : a + b].T, own[a + b : 2 * a + b].T, own[2 * a + b :].T)
    return (token_grad.reshape(tokens.shape), *shares)


def solution(mesh):
    in_specs = (P("dp", "seq", None, None), P("dp", "seq", None, None), P(), P(), P(), P())
    out_specs = (
        P("dp", "seq", None, None),
        P(None, "seq"),
        P(None, "seq"),
        P(None, "seq"),
        P(None, "seq"),
    )
    return jax.shard_map(
        on_device, mesh=mesh, in_specs=in_specs, out_specs=out_specs, check_vma=False
    )
```

```python
import functools

import jax
import jax.numpy as jnp
from jax import lax
from jax.experimental import pallas as pl
from jax.experimental.pallas import tpu as pltpu
from jax.sharding import PartitionSpec as P

HEADS = 6
F32 = jnp.float32
B16 = jnp.bfloat16
NN = (((1,), (0,)), ((), ()))
NT = (((1,), (1,)), ((), ()))
VM = pl.BlockSpec(memory_space=pltpu.VMEM)


def mm(left, right, dims=NN):
    return lax.dot_general(left, right, dims, preferred_element_type=F32)


def normalize(values):
    average = jnp.mean(values, -1, keepdims=True)
    centered = values - average
    spread = jnp.mean(centered * centered, -1, keepdims=True)
    inverse = lax.rsqrt(spread + 1e-06)
    return centered * inverse, inverse


def normalize_back(scaled, inverse, upstream):
    return inverse * (
        upstream
        - jnp.mean(upstream, -1, keepdims=True)
        - scaled * jnp.mean(upstream * scaled, -1, keepdims=True)
    )


def one_head(block, sub, half, rows_axis):
    at = lax.broadcasted_iota(jnp.int32, block.shape, rows_axis)
    keep = (at < half) if sub == 0 else (at >= half)
    return jnp.where(keep, block, jnp.zeros_like(block))


def softmax_rows(scores):
    e = jnp.exp(scores - jnp.max(scores, 0, keepdims=True))
    return (e * (1.0 / jnp.sum(e, 0, keepdims=True))).astype(B16)


def score_back(probs, prob_grad):
    weights = probs.astype(F32)
    total = jnp.sum(weights * prob_grad, 0, keepdims=True)
    return (weights * (prob_grad - total)).astype(B16)


def both_heads(block, half, rows_axis, join_axis):
    return jnp.concatenate(
        [one_head(block, 0, half, rows_axis), one_head(block, 1, half, rows_axis)], join_axis
    )


def regroup(count, inner, outer):
    row = lax.broadcasted_iota(jnp.int32, (count, count), 0)
    column = lax.broadcasted_iota(jnp.int32, (count, count), 1)
    source = (row & (inner - 1)) * outer + lax.shift_right_logical(row, inner.bit_length() - 1)
    return (column == source).astype(F32).astype(B16)


def by_patch(onehot, block, patches):
    size = onehot.shape[0]
    some = size // patches
    moved = [mm(onehot, block[at : at + size]) for at in range(0, block.shape[0], size)]
    return jnp.concatenate(
        [part[p * some : (p + 1) * some] for p in range(patches) for part in moved], 0
    )


def by_frame(onehot, block, patches):
    size = onehot.shape[0]
    some, frames = size // patches, block.shape[0] // patches
    parts = []
    for at in range(0, frames, some):
        rows = [block[p * frames + at : p * frames + at + some] for p in range(patches)]
        parts.append(mm(onehot, jnp.concatenate(rows, 0)))
    return jnp.concatenate(parts, 0)


HBM = pl.BlockSpec(memory_space=pltpu.HBM)


def call(kernel, arrays, outs, in_specs, out_specs, scratch, copies, flops, exps=0, limit=None):
    return pl.pallas_call(
        kernel,
        out_shape=tuple(jax.ShapeDtypeStruct(shape, B16) for shape in outs),
        in_specs=in_specs,
        out_specs=tuple(out_specs),
        scratch_shapes=[pltpu.VMEM(shape, B16) for shape in scratch]
        + [pltpu.SemaphoreType.DMA((copies,))],
        compiler_params=pltpu.CompilerParams(vmem_limit_bytes=limit and limit << 20),
        cost_estimate=pl.CostEstimate(
            flops=flops,
            bytes_accessed=sum(array.size * 2 for array in arrays),
            transcendentals=exps,
        ),
    )(*arrays)


class Copies:
    def __init__(self, sems):
        self.sems, self.pending = sems, []

    def start(self, source, target):
        copy = pltpu.make_async_copy(source, target, self.sems.at[len(self.pending)])
        self.pending.append(copy)
        copy.start()
        return copy


def spatial_forward_kernel(
    tok_hbm, cot_hbm, w_hbm, wo_hbm, slab_ref, saved_hbm,
    tok_ref, cot_ref, w_ref, wo_ref, wide_ref, probs_ref, sems,
):
    copies = Copies(sems)
    tok_in = copies.start(tok_hbm, tok_ref)
    w_in = copies.start(w_hbm, w_ref)
    wo_in = copies.start(wo_hbm, wo_ref)
    cot_in = copies.start(cot_hbm, cot_ref)
    width = tok_ref.shape[-1]
    hw = width // HEADS
    outs = []
    tok_in.wait()
    x = tok_ref[...].astype(F32)
    scaled, _ = normalize(x)
    w_in.wait()
    comb = mm(scaled.astype(B16), w_ref[...]).astype(B16)
    wide_ref[:, : 3 * width] = comb
    rows = comb.shape[0]
    for part in range(2):
        outs.append(
            copies.start(wide_ref.at[:, part * rows : (part + 1) * rows], saved_hbm.at[HEADS + part])
        )
    qt = (comb[:, :width] * (hw ** -0.5)).T
    vt = comb[:, 2 * width :].T

    def scores_of(head):
        at = head // 2 * 2 * hw
        keys = comb[:, width + at : width + at + 2 * hw]
        return mm(keys, one_head(qt[at : at + 2 * hw], head % 2, hw, 0))

    parts, probs = [], []
    ahead = scores_of(0)
    for head in range(HEADS + 1):
        if head < HEADS:
            scores = ahead
            if head + 1 < HEADS:
                ahead = scores_of(head + 1)
            probs.append(softmax_rows(scores))
            probs_ref[head] = probs[head]
            outs.append(copies.start(probs_ref.at[head], saved_hbm.at[head]))
        if head:
            own = slice((head - 1) * hw, head * hw)
            parts.append(mm(vt[own], probs[head - 1]).astype(B16))
    att = jnp.concatenate(parts, 0).T
    wide_ref[:, 3 * width :] = att
    outs.append(copies.start(wide_ref.at[:, 2 * rows :], saved_hbm.at[HEADS + 2]))
    wo_in.wait()
    out = (x + mm(att, wo_ref[...])).astype(B16)
    cot_in.wait()
    half = (slab_ref.shape[0],) + slab_ref.shape[2:]
    slab_ref[:, 0] = out.reshape(half)
    slab_ref[:, 1] = cot_ref[...].reshape(half)
    for copy in outs:
        copy.wait()


def spatial_forward(tokens, cotangent, w, wo, slab):
    rows, width = tokens.shape
    wide, square = (rows, 4 * width), (rows, width)
    return call(
        spatial_forward_kernel, (tokens, cotangent, w, wo),
        (slab, (HEADS + 3, rows, rows)), [HBM] * 4, [VM, HBM],
        [square, square, w.shape, wo.shape, wide, (HEADS, rows, rows)],
        7 + HEADS, 2_000_000_000, 1_600_000, None,
    )


def temporal_kernel(
    factor, slab_ref, w_ref, wo_ref, branch_ref, normed_ref, go_ref, dct_ref, sems,
):
    frames, _, patches, width = slab_ref.shape
    rows = frames * patches
    hw = width // HEADS
    size = min(rows, 256)
    gather = regroup(size, size // patches, patches)
    x = by_patch(gather, slab_ref[:, 0].reshape(rows, width), patches)
    cot = by_patch(gather, slab_ref[:, 1].reshape(rows, width), patches).astype(B16)
    scaled, inverse = normalize(x)
    normed = scaled.astype(B16)
    normed_ref[...] = normed
    comb = mm(normed, w_ref[...]).astype(B16)
    g = mm(cot, wo_ref[...], NT).astype(B16)
    q = comb[:, :width] * (hw ** -0.5)
    k = comb[:, width : 2 * width]
    v = comb[:, 2 * width :]
    qt, kt, vt, gt = q.T, k.T, v.T, g.T
    groups = [
        (slice(patch * frames, (patch + 1) * frames), slice(pair * 2 * hw, (pair + 1) * 2 * hw))
        for patch in range(patches)
        for pair in range(HEADS // 2)
    ]
    scores = [mm(k[here, lanes], both_heads(qt[lanes, here], hw, 0, 1)) for here, lanes in groups]
    back = [mm(v[here, lanes], both_heads(gt[lanes, here], hw, 0, 1)) for here, lanes in groups]
    probs = [softmax_rows(member) for member in scores]
    grads = [score_back(p, dp) for p, dp in zip(probs, back)]
    dk = [mm(ds, both_heads(q[at], hw, 1, 0)).astype(B16) for ds, at in zip(grads, groups)]
    dv = [mm(p, both_heads(g[at], hw, 1, 0)).astype(B16) for p, at in zip(probs, groups)]
    att, dqt = [], []
    for p, ds, (here, lanes) in zip(probs, grads, groups):
        for sub in range(2):
            own = slice(lanes.start + sub * hw, lanes.start + (sub + 1) * hw)
            cols = slice(sub * frames, (sub + 1) * frames)
            att.append(mm(vt[own, here], p[:, cols]).astype(B16))
            dqt.append((mm(kt[own, here], ds[:, cols]) * (hw ** -0.5)).astype(B16))

    def by_patch_of(parts, axis):
        each = len(parts) // patches
        return [
            jnp.concatenate(parts[n * each : (n + 1) * each], axis) for n in range(patches)
        ]

    dqt_parts, att_parts = by_patch_of(dqt, 0), by_patch_of(att, 0)
    dk_parts, dv_parts = by_patch_of(dk, 1), by_patch_of(dv, 1)
    dqt = jnp.concatenate(dqt_parts, 1)
    att = jnp.concatenate(att_parts, 1).T
    go_ref[...] = (mm(cot.T, att) * factor).astype(B16)
    dk = jnp.concatenate(dk_parts, 0)
    dv = jnp.concatenate(dv_parts, 0)
    dct_ref[:width] = dqt
    dct_ref[width : 2 * width] = dk.T
    dct_ref[2 * width :] = dv.T
    u = (
        mm(dqt.T, w_ref[:, :width], NT)
        + mm(dk, w_ref[:, width : 2 * width], NT)
        + mm(dv, w_ref[:, 2 * width :], NT)
    )
    branch = normalize_back(scaled, inverse, u).astype(B16)
    scatter = regroup(size, patches, size // patches)
    branch = by_frame(scatter, branch, patches).astype(B16)
    branch_ref[...] = branch.reshape(branch_ref.shape)


def temporal(factor, slab, w, wo):
    frames, _, patches, width = slab.shape
    rows = frames * patches
    return call(
        functools.partial(temporal_kernel, factor), (slab, w, wo),
        ((frames, patches, width), (rows, width), wo.shape, (3 * width, rows)),
        [VM] * 3, [VM] * 4, [], 1, 3_000_000_000, 400_000, 48,
    )


def exchange_order(cores, depth, rows, a, b):
    each = a + b
    pair = rows // each
    row = lax.broadcasted_iota(jnp.int32, (cores * depth * rows, 1), 0)
    slab = lax.shift_right_logical(row * ((1 << 16) // each + 1), 16)
    i = row - slab * each
    yh = slab & (pair - 1)
    z = lax.shift_right_logical(slab, pair.bit_length() - 1) & (depth - 1)
    core = lax.shift_right_logical(slab, (pair * depth).bit_length() - 1)
    member = (yh * depth + z) * cores + core
    source = jnp.where(i < a, member * a + i, cores * depth * pair * a + member * b + i - a)
    column = lax.broadcasted_iota(jnp.int32, (row.shape[0], row.shape[0]), 1)
    return (column == source).astype(F32).astype(B16)


def spread(gq, go, slab_ref, own_ref, send_ref):
    here = lax.axis_index("seq") % slab_ref.shape[0]
    groups = slab_ref.shape[1]
    a, b = gq.shape[0] // groups, go.shape[0] // groups
    cores, _, depth, rows, _ = slab_ref.shape
    each = a // (cores * depth * 2), b // (cores * depth * 2)
    onehot = exchange_order(cores, depth, rows, *each)
    for x in range(groups):
        source = jnp.concatenate([gq[x * a : (x + 1) * a], go[x * b : (x + 1) * b]], 0)
        moved = mm(onehot, source).astype(B16)
        slab_ref[:, x] = moved.reshape(slab_ref.shape[:1] + slab_ref.shape[2:])
        send_ref[x] = slab_ref[1 - here, x]
        own_ref[x] = slab_ref[here, x]


def weight_kernel(factor, normed_ref, go_ref, dct_ref, own_ref, send_ref, slab_ref, _):
    gq = (mm(dct_ref[...], normed_ref[...]) * factor).astype(B16)
    spread(gq, go_ref[...], slab_ref, own_ref, send_ref)


def weight_slabs(factor, normed, go, dct, shape):
    return call(
        functools.partial(weight_kernel, factor), (normed, go, dct),
        (shape[1:], shape[1:]), [VM] * 3, [VM] * 2, [shape], 1, 1_500_000_000, 0, 48,
    )


def spatial_backward_kernel(
    factor, ct_ref, br_ref, wo_ref, saved_hbm, tok_ref,
    own_ref, send_ref, sg_ref, dqt_ref, dkv_ref,
    comb_ref, probs_ref, slab_ref, sems,
):
    copies = Copies(sems)
    rows, width = ct_ref.shape
    comb_in = [
        copies.start(saved_hbm.at[HEADS + part], comb_ref.at[:, part * rows : (part + 1) * rows])
        for part in (2, 0, 1)
    ]
    probs_in = [copies.start(saved_hbm.at[h], probs_ref.at[h]) for h in range(HEADS)]
    hw = width // HEADS
    branch = br_ref[...].reshape(rows, width)
    sg = (ct_ref[...].astype(F32) + branch.astype(F32)).astype(B16)
    sg_ref[...] = sg
    g = mm(sg, wo_ref[...], NT).astype(B16)
    gt = g.T
    scaled, _ = normalize(tok_ref[...].astype(F32))
    normed = scaled.astype(B16)
    for copy in comb_in:
        copy.wait()
    go = (mm(sg.T, comb_ref[:, 3 * width :]) * factor).astype(B16)
    q = comb_ref[:, :width] * (hw ** -0.5)
    kt = comb_ref[:, width : 2 * width].T

    def back_of(head):
        at = head // 2 * 2 * hw
        values = comb_ref[:, 2 * width + at : 2 * width + at + 2 * hw]
        return mm(values, one_head(gt[at : at + 2 * hw], head % 2, hw, 0))

    dqt_parts, dk_parts, dv_parts, grads = [], [], [], []
    ahead = back_of(0)
    for copy in probs_in:
        copy.wait()
    for step in range(HEADS + 1):
        if step < HEADS:
            dp = ahead
            if step + 1 < HEADS:
                ahead = back_of(step + 1)
            grads.append(score_back(probs_ref[step], dp))
        if not step:
            continue
        head, sub = step - 1, (step - 1) % 2
        lanes = slice(head // 2 * 2 * hw, (head // 2 + 1) * 2 * hw)
        ds = grads[head]
        dqt = mm(kt[head * hw : (head + 1) * hw], ds) * (hw ** -0.5)
        dqt_parts.append(dqt.astype(B16))
        dk = mm(ds, one_head(q[:, lanes], sub, hw, 1))
        dv = mm(probs_ref[head], one_head(g[:, lanes], sub, hw, 1))
        if sub:
            dk_parts.append((dk_first + dk).astype(B16))
            dv_parts.append((dv_first + dv).astype(B16))
        dk_first, dv_first = dk, dv
    dqt = jnp.concatenate(dqt_parts, 0)
    dk = jnp.concatenate(dk_parts, 1)
    dv = jnp.concatenate(dv_parts, 1)
    dct = jnp.concatenate([dqt, dk.T, dv.T], 0)
    gq = (mm(dct, normed) * factor).astype(B16)
    spread(gq, go, slab_ref, own_ref, send_ref)
    dqt_ref[...] = dqt
    dkv_ref[:, :width] = dk
    dkv_ref[:, width:] = dv


def spatial_backward(factor, ct, branch, wo, saved, tokens, shape):
    rows, width = tokens.shape
    arrays = (ct, branch, wo, saved, tokens)
    square, wide = (rows, width), (rows, 2 * width)
    return call(
        functools.partial(spatial_backward_kernel, factor), arrays,
        (shape[1:], shape[1:], square, (width, rows), wide),
        [VM, VM, VM, HBM, VM], [VM] * 5,
        [(rows, 4 * width), (HEADS, rows, rows), shape], 3 + HEADS, 4_000_000_000, 0, 48,
    )


def token_kernel(tok_ref, w_ref, dqt_ref, dkv_ref, sg_ref, out_ref, _):
    width = tok_ref.shape[1]
    scaled, inverse = normalize(tok_ref[...].astype(F32))
    u = mm(dqt_ref[...].T, w_ref[:, :width], NT) + mm(dkv_ref[...], w_ref[:, width:], NT)
    out_ref[...] = (sg_ref[...].astype(F32) + normalize_back(scaled, inverse, u)).astype(B16)


def token_gradient(tokens, w, dqt, dkv, sg):
    return call(
        token_kernel, (tokens, w, dqt, dkv, sg), (tokens.shape,),
        [VM] * 5, [VM], [], 1, 500_000_000, 0, 48,
    )[0]


SEQ = (("x", 4), ("yh", 2), ("z", 8), ("core", 2))


def seq_size():
    return lax.axis_size("seq")


def place(name):
    stride = 1
    for member, size in reversed(SEQ):
        if member == name:
            return stride, size
        stride *= size


def coordinate(name):
    stride, size = place(name)
    return lax.axis_index("seq") // stride % size


def shift(array, name, step):
    stride, size = place(name)
    pairs = []
    for index in range(seq_size()):
        at = index // stride % size
        pairs.append((index, index + ((at + step) % size - at) * stride))
    return lax.ppermute(array, "seq", pairs)


def slab_shape(width):
    sizes = dict(SEQ)
    rows = sizes["yh"] * 4 * width // seq_size()
    return (sizes["core"], sizes["x"], sizes["z"], rows, width)


def total_of(refs):
    here = coordinate("x")
    total = refs[0][here].astype(F32)
    for ref in refs[1:]:
        total = total + ref[...].astype(F32)
    return total.astype(B16)


def sum_kernel(*refs):
    refs[-2][...] = total_of(refs[:-2])


def join_kernel(early_ref, *refs):
    out_ref = refs[-2]
    late, early = total_of(refs[:-2]), early_ref[...]
    pair, rows = out_ref.shape[0], out_ref.shape[2] // 2
    for yh in range(pair):
        part = slice(yh * rows, (yh + 1) * rows)
        out_ref[yh] = jnp.concatenate([late[:, part], early[:, part]], 1)


def first_stages(own, send):
    part = (own.astype(F32) + shift(send, "core", 1).astype(F32)).astype(B16)
    here, size = coordinate("x"), part.shape[0]
    return (part,) + tuple(
        shift(lax.dynamic_index_in_dim(part, (here + k) % size, 0, keepdims=False), "x", k)
        for k in sorted(range(1, size), key=lambda k: -min(k, size - k))
    )


def sum_early(parts):
    return call(
        sum_kernel, parts, (parts[0].shape[1:],), [VM] * len(parts), [VM], [],
        1, 1_000_000, 0, 48,
    )[0]


def join(early, parts):
    z, rows, width = early.shape
    return call(
        join_kernel, (early, *parts), ((2, z, rows, width),), [VM] * (1 + len(parts)),
        [VM], [], 1, 1_000_000, 0, 48,
    )[0]


def groups_of(*names):
    wanted = [place(name) for name in names]
    groups = []
    for index in range(seq_size()):
        if all(index // stride % size == 0 for stride, size in wanted):
            members = [index]
            for stride, size in wanted:
                members = [at + k * stride for at in members for k in range(size)]
            groups.append(members)
    return groups


def last_stages(part):
    yh, z = part.shape[:2]
    flat = part.reshape(yh * z, *part.shape[2:])
    got = lax.all_to_all(
        flat, "seq", split_axis=0, concat_axis=0, tiled=True, axis_index_groups=groups_of("yh", "z")
    )
    mine = jnp.sum(got.astype(F32), 0).astype(B16)
    return mine, lax.ppermute(mine, "dp", [(0, 1), (1, 0)])


def share_kernel(mine_ref, other_ref, *out_refs):
    total = mine_ref[...].astype(F32) + other_ref[...].astype(F32)
    start = 0
    for ref in out_refs:
        ref[...] = total[start : start + ref.shape[0]]
        start += ref.shape[0]


def shares_of(mine, other, counts):
    return pl.pallas_call(
        share_kernel,
        out_shape=tuple(jax.ShapeDtypeStruct((n, mine.shape[1]), F32) for n in counts),
        in_specs=[VM] * 2,
        out_specs=(VM,) * len(counts),
        compiler_params=pltpu.CompilerParams(vmem_limit_bytes=48 << 20),
        name="shares",
    )(mine, other)


def on_device(tokens, cotangent, wqkv_spatial, wo_spatial, wqkv_temporal, wo_temporal):
    clips, frames, patches, width = tokens.shape
    factor = (clips * frames * patches * lax.axis_size("dp") * seq_size()) ** (-0.5)
    shape = slab_shape(width)
    tok = tokens.reshape(patches, width)
    cot = cotangent.reshape(patches, width)
    traded = (seq_size(), 2, patches // seq_size(), width)

    def trade(array):
        return lax.all_to_all(array, "seq", split_axis=0, concat_axis=0, tiled=True)

    stream, saved = spatial_forward(tok, cot, wqkv_spatial, wo_spatial, traded)
    branch, normed_t, go_t, dct = temporal(factor, trade(stream), wqkv_temporal, wo_temporal)
    branch = trade(branch)
    own, send = weight_slabs(factor, normed_t, go_t, dct, shape)
    half_t = first_stages(own, send)
    own, send, stream_grad, dqt, dkv = spatial_backward(
        factor, cot, branch, wo_spatial, saved, tok, shape
    )
    half_s = first_stages(own, send)
    token_grad = token_gradient(tok, wqkv_spatial, dqt, dkv, stream_grad)
    half_t = sum_early(half_t)
    joined = join(half_t, half_s)
    mine, other = last_stages(joined)
    a, b = 3 * width // seq_size(), width // seq_size()
    shares = [share.T for share in shares_of(mine, other, (a, b, a, b))]
    return (token_grad.reshape(tokens.shape), *shares)


def solution(mesh):
    in_specs = (P("dp", "seq", None, None), P("dp", "seq", None, None), P(), P(), P(), P())
    out_specs = (
        P("dp", "seq", None, None),
        P(None, "seq"),
        P(None, "seq"),
        P(None, "seq"),
        P(None, "seq"),
    )
    return jax.shard_map(
        on_device, mesh=mesh, in_specs=in_specs, out_specs=out_specs, check_vma=False
    )
```
